512 devices in a mesh: stu: 16 (over z_lo, x), que: 32 (over z_hi, y, core).
Axes of the slice: x: 4, y: 8, z: 8 (z_hi: 2, z_lo: 4; z = z_hi * 4 + z_lo), core: 2. Of those that a mesh axis runs over, the one named last changes fastest.
Arguments:
- codes: int32 [4096, 4096], P('stu', 'que'), may hold values from 0 to 2
- theta: float32 [4096, 64], P(('stu', 'que')), may hold values from -6 to 6
- disc: float32 [4096, 64], P(('que', 'stu')), may hold values from -0.75 to 0.75
- intercept: float32 [4096], P(('que', 'stu')), may hold values from -5 to 5
Outputs:
- step_abilities: float32 [4096, 64], P(('stu', 'que'))
- step_disc: float32 [4096, 64], P(('que', 'stu'))
- step_intercept: float32 [4096], P(('que', 'stu'))
The draws below stay inside these ranges and needn't reach their ends.
All inputs are finite; a program needn't handle non-finite values.
Results may differ from the reference program's by a relative error of at most 0.0003.
Values sent between devices are 32-bit elements; how exact they have to be, the bound alone decides.
A program may use at most 64 MiB of HBM per device.

```python
import jax
import jax.numpy as jnp
from jax import lax

K = 64
TILE_S = 256
ITERS = 2
STUDENTS = 4096
QUESTIONS = 4096
N_STU = 16


def with_ends(entries, stream_key, least, high):
    dims = entries.shape
    index_at = [jax.random.randint(jax.random.fold_in(stream_key, axis), (), 0, dims[axis]) for axis in range(len(dims))]
    entries = entries.at[tuple(index_at)].set(least)
    longest = dims.index(max(dims))
    index_at[longest] = (index_at[longest] + 1) % dims[longest]
    return entries.at[tuple(index_at)].set(high)


def levels(stream_key, extent, cuts, least, high):
    gain = 1.0
    for position, shards_of in cuts:
        steps = jax.random.uniform(jax.random.fold_in(jax.random.fold_in(stream_key, 6), position), (shards_of,), jnp.float32, least / len(cuts), high / len(cuts))
        gain = gain * jnp.repeat(jnp.exp(steps), extent[position] // shards_of).reshape((-1,) + (1,) * (len(extent) - 1 - position))
    return gain


def normal_values(stream_key, extent, scale, limit, cuts=(), dtype=jnp.bfloat16):
    values = scale * jax.random.normal(stream_key, extent, jnp.float32)
    if cuts:
        values = values * levels(stream_key, extent, cuts, -0.22, 0.18)
    return jnp.clip(values, -limit, limit).astype(dtype)


def setup_inputs(seed: int = 0) -> dict:
    splits = jax.random.split(jax.random.key(seed), 5)
    return {
        "codes": with_ends(jax.random.randint(splits[0], (STUDENTS, QUESTIONS), 0, 3), jax.random.fold_in(splits[0], 1), 0, 2).astype(jnp.int32),
        "theta": normal_values(splits[1], (STUDENTS, K), 1.0, 6.0, ((0, 512),), jnp.float32),
        "disc": normal_values(splits[2], (QUESTIONS, K), K ** -0.5, 0.75, ((0, 512),), jnp.float32),
        "intercept": normal_values(splits[3], (QUESTIONS,), 1.0, 5.0, ((0, 512),), jnp.float32),
    }


HIGH = lax.Precision.HIGHEST

def matmul(left, right):
    return jnp.dot(left, right, precision=HIGH, preferred_element_type=jnp.float32)

def contract_rows(left, right):
    return lax.dot_general(left, right, (((0,), (0,)), ((), ())), precision=HIGH, preferred_element_type=jnp.float32)

def block_terms(code_blk, theta_blk, disc, intercept):
    logit = matmul(theta_blk, disc.T) + intercept[None, :]
    prob = jax.nn.sigmoid(logit)
    observed = (code_blk > 0).astype(jnp.float32)
    correct = (code_blk == 2).astype(jnp.float32)
    return (observed * (prob - correct), observed * prob * (1.0 - prob))

def reference(codes, theta, disc, intercept):
    blocks = codes.reshape(N_STU, TILE_S, QUESTIONS)
    theta_blocks = theta.reshape(N_STU, TILE_S, K)
    zero_cols = (jnp.zeros((QUESTIONS, K), jnp.float32), jnp.zeros((QUESTIONS, K), jnp.float32), jnp.zeros((QUESTIONS,), jnp.float32), jnp.zeros((QUESTIONS,), jnp.float32))

    def grad_step(carry, item):
        code_blk, theta_blk = item
        resid, weight = block_terms(code_blk, theta_blk, disc, intercept)
        rows = (matmul(resid, disc), matmul(weight, disc * disc))
        cols = (contract_rows(resid, theta_blk), contract_rows(weight, theta_blk * theta_blk), lax.optimization_barrier(jnp.sum(resid, 0)), lax.optimization_barrier(jnp.sum(weight, 0)))
        return (jax.tree.map(lambda u, v: u + v, carry, cols), rows)
    cols, rows = lax.scan(grad_step, zero_cols, (blocks, theta_blocks))
    grad = (rows[0].reshape(STUDENTS, K) + theta, cols[0] + disc, cols[2] + intercept)
    diag = (rows[1].reshape(STUDENTS, K) + 1.0, cols[1] + 1.0, cols[3] + 1.0)

    def apply_hessian(vec):
        vt_blocks = vec[0].reshape(N_STU, TILE_S, K)

        def hess_step(carry, item):
            code_blk, theta_blk, vt_blk = item
            resid, weight = block_terms(code_blk, theta_blk, disc, intercept)
            change = matmul(vt_blk, disc.T) + matmul(theta_blk, vec[1].T) + vec[2][None, :]
            scaled = weight * change
            cols_now = (contract_rows(scaled, theta_blk), lax.optimization_barrier(jnp.sum(scaled, 0)))
            return ((carry[0] + cols_now[0], carry[1] + cols_now[1]), matmul(scaled, disc))
        start = (jnp.zeros((QUESTIONS, K), jnp.float32), jnp.zeros((QUESTIONS,), jnp.float32))
        col_part, row_part = lax.scan(hess_step, start, (blocks, theta_blocks, vt_blocks))
        return (row_part.reshape(STUDENTS, K) + vec[0], col_part[0] + vec[1], col_part[1] + vec[2])

    def inner(left, right):
        return jnp.sum(left[0] * right[0]) + jnp.sum(left[1] * right[1]) + jnp.sum(left[2] * right[2])
    solution = jax.tree.map(jnp.zeros_like, grad)
    residual = jax.tree.map(lambda u: -u, grad)
    precond = jax.tree.map(lambda u, d: u / d, residual, diag)
    direction = precond
    norm_now = inner(residual, precond)
    for step in range(ITERS):
        image = apply_hessian(direction)
        alpha = norm_now / inner(direction, image)
        solution = jax.tree.map(lambda u, v: u + alpha * v, solution, direction)
        residual = jax.tree.map(lambda u, v: u - alpha * v, residual, image)
        if step + 1 < ITERS:
            precond = jax.tree.map(lambda u, d: u / d, residual, diag)
            norm_next = inner(residual, precond)
            ratio = norm_next / norm_now
            direction = jax.tree.map(lambda u, v: u + ratio * v, precond, direction)
            norm_now = norm_next
    result = jax.tree.map(lambda u, d: u * jnp.sqrt(d), solution, diag)
    return (result[0], result[1], result[2])
```

```python
import functools

import jax
import jax.numpy as jnp
from jax import lax
from jax.experimental import pallas as pl
from jax.experimental.pallas import tpu as pltpu
from jax.sharding import PartitionSpec as P

DIMS = dict(ZL=4, X=4, ZH=2, Y=8, C=2)
K = 64
W = 128
MESH = pl.DeviceIdType.MESH
F32 = jnp.float32
HIGH = lax.Precision.HIGHEST


def dot_nn(a, b):
    return lax.dot_general(a, b, (((1,), (0,)), ((), ())), precision=HIGH, preferred_element_type=F32)


def dot_nt(a, b):
    return lax.dot_general(a, b, (((1,), (1,)), ((), ())), precision=HIGH, preferred_element_type=F32)


def dot_tn(a, b):
    return lax.dot_general(a, b, (((0,), (0,)), ((), ())), precision=HIGH, preferred_element_type=F32)


def tree_sum(parts):
    parts = list(parts)
    while len(parts) > 1:
        parts = [parts[i] + parts[i + 1] if i + 1 < len(parts) else parts[i] for i in range(0, len(parts), 2)]
    return parts[0]


def kernel(dims, names, codes_hbm, theta_ref, disc_ref, icpt_ref, out_t, out_d, out_b, codes_v, *rest):
    ZL, X, ZH, Y, C = (dims[n] for n in ("ZL", "X", "ZH", "Y", "C"))
    ref = dict(zip(names, rest))
    ssem, rsem, lsem = rest[len(names):]
    stu, que = lax.axis_index("stu"), lax.axis_index("que")
    zl, x = stu // X, stu % X
    zh, y, core = que // (Y * C), (que // C) % Y, que % C
    half = ZL // 2
    zq, zr = zl // half, zl % half
    Q = ZL * X * 8
    YB, XB = C * 8, half * 8
    SH = Y * YB
    NXY, NZC = X * Y, ZL * ZH * C

    def at(zl_, x_, zh_, y_, core_):
        return (zl_ * X + x_, (zh_ * Y + y_) * C + core_)

    def dev_y(k):
        return at(zl, x, zh, jnp.bitwise_xor(y, k), core)

    def dev_x(k):
        return at(zl, jnp.bitwise_xor(x, k), zh, y, core)

    def dev_hc(k):
        return at(zl, x, jnp.bitwise_xor(zh, k // C), y, jnp.bitwise_xor(core, k % C))

    def dev_l(k):
        return at(jnp.bitwise_xor(zl, k), x, zh, y, core)

    def dev_xy(k):
        return at(zl, jnp.bitwise_xor(x, k // Y), zh, jnp.bitwise_xor(y, k % Y), core)

    def dev_zc(k):
        return at(
            jnp.bitwise_xor(zl, k // (ZH * C)), x, jnp.bitwise_xor(zh, (k // C) % ZH), y, jnp.bitwise_xor(core, k % C)
        )

    index_of = {n: i for i, n in enumerate(names)}
    sent = []

    def send(src, name, slot, device):
        pltpu.make_async_remote_copy(
            src_ref=src,
            dst_ref=ref[name].at[slot],
            send_sem=ssem.at[index_of[name]],
            recv_sem=rsem.at[index_of[name]],
            device_id=device,
            device_id_type=MESH,
        ).start()

    def spread(name, count, dev):
        for k in range(1, count):
            send(ref[name].at[0], name, k, dev(k))
        sent.append((name, 1, count))

    def spread_loop(name, count, dev):
        def one(k, carry):
            send(ref[name].at[0], name, k, dev(k))
            return carry
        lax.fori_loop(1, count, one, 0)
        sent.append((name, 1, count))

    def scatter(src, name, count, me, dev):
        for k in range(1, count):
            send(ref[src].at[jnp.bitwise_xor(me, k)], name, k - 1, dev(k))
        sent.append((name, 0, count - 1))

    def arrived(name, lo, hi):
        r = ref[name].at[pl.ds(lo, hi - lo)]
        pltpu.make_async_copy(r, r, rsem.at[index_of[name]]).wait()

    def total(name, count):
        return tree_sum(ref[name][k] for k in range(count))

    fetch = pltpu.make_async_copy(codes_hbm, codes_v, lsem)
    fetch.start()

    barrier = pltpu.get_barrier_semaphore()

    def greet(dev):
        def one(k, carry):
            pl.semaphore_signal(barrier, inc=1, device_id=dev(k), device_id_type=MESH)
            return carry
        return one
    lax.fori_loop(1, NZC, greet(dev_zc), 0)
    lax.fori_loop(1, NXY, greet(dev_xy), 0)

    low8 = lax.broadcasted_iota(jnp.int32, (8, W), 1) // K
    th, dc = theta_ref[...], disc_ref[...]
    ref["t1"][0] = jnp.where(low8 == zh, jnp.concatenate([th, th], 1), 0.0)
    ref["d1"][0] = jnp.where(low8 == zq, jnp.concatenate([dc, dc], 1), 0.0)
    qlane = lax.broadcasted_iota(jnp.int32, (1, Q), 1)
    brow = jnp.zeros((1, Q), F32)
    for k in range(8):
        brow = jnp.where(qlane == stu * 8 + k, icpt_ref[k], brow)
    ref["b1"][0] = brow

    pl.semaphore_wait(barrier, NXY + NZC - 2)

    spread("t1", ZH * C, dev_hc)
    spread("d1", ZL, dev_l)
    spread("b1", ZL, dev_l)

    arrived("d1", 1, ZL)
    slot_l = lambda z: jnp.bitwise_xor(zl, z)
    d_own = jnp.concatenate([ref["d1"][slot_l(r)] + ref["d1"][slot_l(half + r)] for r in range(half)], 0)
    ref["d2"][0] = d_own
    spread("d2", X, dev_x)
    arrived("b1", 1, ZL)
    ref["b2"][0] = total("b1", ZL)
    spread("b2", X, dev_x)
    arrived("t1", 1, ZH * C)
    slot_hc = lambda h, c: jnp.bitwise_xor(zh, h) * C + jnp.bitwise_xor(core, c)
    t_own = jnp.concatenate([ref["t1"][slot_hc(0, c)] + ref["t1"][slot_hc(1, c)] for c in range(C)], 0)
    ref["t2"][0] = t_own
    spread("t2", Y, dev_y)

    def rows_of(name):
        return jnp.concatenate([ref[name][jnp.bitwise_xor(y, k)] for k in range(Y)], 0)

    def low(v):
        return lax.broadcasted_iota(jnp.int32, v.shape, 1) < K

    def swap(v):
        return pltpu.roll(v, K, 1)

    def cols_of(name):
        packed = jnp.concatenate(
            [ref[name][jnp.bitwise_xor(x, k), pl.ds(r * 8, 8)] for r in range(half) for k in range(X)], 0
        )
        turned = swap(packed)
        lo = low(packed)
        zero = jnp.zeros_like(packed)
        first = jnp.concatenate([jnp.where(lo, packed, zero), jnp.where(lo, turned, zero)], 0)
        second = jnp.concatenate([jnp.where(lo, zero, turned), jnp.where(lo, zero, packed)], 0)
        return first, second

    def pack_cols(v):
        upper, lower = v[: Q // 2], v[Q // 2 :]
        return jnp.where(low(upper), upper, lower)

    arrived("d2", 1, X)
    dd = cols_of("d2")
    arrived("b2", 1, X)
    bias = total("b2", X)
    fetch.wait()
    arrived("t2", 1, Y)
    theta = rows_of("t2")
    turned = swap(theta)
    lo = low(theta)
    tt = (jnp.where(lo, theta, turned), jnp.where(lo, turned, theta))

    resid, weight = [], []
    for h in range(ZH):
        prob = jax.nn.sigmoid(dot_nt(theta, dd[h]) + bias)
        code = codes_v[pl.ds(h * SH, SH)]
        observed = (code > 0).astype(F32)
        correct = (code == 2).astype(F32)
        resid.append(observed * (prob - correct))
        weight.append(observed * prob * (1.0 - prob))

    def row_part(u, d):
        return dot_nn(u[0], d[0]) + dot_nn(u[1], d[1])

    def col_part(u, t):
        return pack_cols(dot_tn(u[0], t[0]) + dot_tn(u[1], t[1]))

    def col_sum(u):
        return jnp.sum(u[0], 0, keepdims=True) + jnp.sum(u[1], 0, keepdims=True)

    def put_rows(name, offset, v):
        for k in range(Y):
            ref[name][k, pl.ds(offset, YB)] = v[k * YB : (k + 1) * YB]

    def put_cols(name, offset, v):
        for k in range(X):
            for r in range(half):
                start = (r * X + k) * 8
                ref[name][k, pl.ds(offset + r * 8, 8)] = v[start : start + 8]

    def reduce_all(tag, row_list, col_list, sums, during_first=None, during_second=None):
        for i, v in enumerate(row_list):
            put_rows("ra" + tag, i * YB, v)
        scatter("ra" + tag, "rb" + tag, Y, y, dev_y)
        for i, v in enumerate(col_list):
            put_cols("ca" + tag, i * XB, v)
        scatter("ca" + tag, "cb" + tag, X, x, dev_x)
        ref["sa" + tag][0] = sums
        spread("sa" + tag, X, dev_x)
        if during_first is not None:
            during_first()
        arrived("cb" + tag, 0, X - 1)
        ref["cc" + tag][0] = tree_sum([ref["ca" + tag][x]] + [ref["cb" + tag][k] for k in range(X - 1)])
        spread("cc" + tag, ZL, dev_l)
        arrived("sa" + tag, 1, X)
        ref["sb" + tag][0] = total("sa" + tag, X)
        spread("sb" + tag, ZL, dev_l)
        arrived("rb" + tag, 0, Y - 1)
        ref["rc" + tag][0] = tree_sum([ref["ra" + tag][y]] + [ref["rb" + tag][k] for k in range(Y - 1)])
        spread("rc" + tag, ZH * C, dev_hc)
        if during_second is not None:
            during_second()
        arrived("cc" + tag, 1, ZL)
        cols = total("cc" + tag, ZL)
        arrived("sb" + tag, 1, ZL)
        sums = total("sb" + tag, ZL)
        arrived("rc" + tag, 1, ZH * C)
        rows = total("rc" + tag, ZH * C)
        return rows, cols, sums

    def gather_start(tag, rows, cols):
        ref["rg" + tag][0] = rows
        spread("rg" + tag, Y, dev_y)
        ref["cg" + tag][0] = cols
        spread("cg" + tag, X, dev_x)

    def change_of(tag, vb):
        arrived("cg" + tag, 1, X)
        va = cols_of("cg" + tag)
        arrived("rg" + tag, 1, Y)
        left = jnp.concatenate([rows_of("rg" + tag), theta], 1)
        return [dot_nt(left, jnp.concatenate([dd[h], va[h]], 1)) + vb for h in range(ZH)]

    def lanes(v):
        s = jnp.sum(v, 0, keepdims=True)
        if s.shape[1] < W:
            s = jnp.concatenate([s, jnp.zeros((1, W - s.shape[1]), F32)], 1)
        return s

    def inner(u, v):
        rows = lanes(u[0] * v[0]) * (1.0 / (ZH * C))
        cols = lanes(u[1] * v[1]) * (1.0 / ZL)
        return rows + cols + lanes(u[2] * v[2]) * (1.0 / (ZL * X))

    def first_round(tag, values):
        for i, v in enumerate(values):
            ref["p" + tag][0, pl.ds(i, 1)] = v
        spread_loop("p" + tag, NXY, dev_xy)

    def second_round(tag):
        arrived("p" + tag, 1, NXY)
        ref["q" + tag][0] = jnp.sum(ref["p" + tag][...], 0)
        spread_loop("q" + tag, NZC, dev_zc)

    def last_round(tag):
        arrived("q" + tag, 1, NZC)
        return jnp.sum(jnp.sum(ref["q" + tag][...], 0), 1, keepdims=True)

    d2 = [d * d for d in dd]
    t2 = [t * t for t in tt]
    sums = jnp.concatenate([col_sum(resid), col_sum(weight)], 0)
    rows, cols, sums = reduce_all(
        "1",
        (row_part(resid, dd), row_part(weight, d2)),
        (col_part(resid, tt), col_part(weight, t2)),
        sums,
    )
    r = (-(rows[:YB] + t_own), -(cols[:XB] + d_own), -(sums[0:1] + bias))
    dg = (rows[YB:] + 1.0, cols[XB:] + 1.0, sums[1:2] + 1.0)
    z = [a / b for a, b in zip(r, dg)]
    gather_start("1", z[0], z[1])
    rz_part = inner(r, z)
    zz_part = inner(z, z)
    change = change_of("1", z[2])
    scaled = [w * c for w, c in zip(weight, change)]
    pq_part = lanes(scaled[0] * change[0]) + lanes(scaled[1] * change[1]) + zz_part

    rows, cols, sums = reduce_all(
        "2",
        (row_part(scaled, dd),),
        (col_part(scaled, tt),),
        col_sum(scaled),
        during_first=lambda: first_round("1", (rz_part, pq_part)),
        during_second=lambda: second_round("1"),
    )
    image = (rows + z[0], cols + z[1], sums + z[2])
    scalars = last_round("1")
    rz, pq = scalars[0:1], scalars[1:2]
    alpha = rz / pq
    r = [a - alpha * b for a, b in zip(r, image)]
    z_next = [a / b for a, b in zip(r, dg)]
    gather_start("2", z_next[0], z_next[1])
    first_round("2", (inner(r, z_next),))
    change_next = change_of("2", z_next[2])
    second_round("2")
    new = last_round("2")
    beta = new / rz
    p = [a + beta * b for a, b in zip(z_next, z)]
    change = [a + beta * b for a, b in zip(change_next, change)]
    curv = inner(p, p)
    for w, c in zip(weight, change):
        curv = curv + lanes(w * c * c)
    first_round("3", (curv,))
    second_round("3")
    alpha_two = new / last_round("3")
    step = [(alpha * a + alpha_two * b) * jnp.sqrt(d) for a, b, d in zip(z, p, dg)]

    ref["xt"][...] = step[0]
    mine = ref["xt"][pl.ds(pl.multiple_of(core * 8, 8), 8)]
    out_t[...] = jnp.where(zh == 0, mine, swap(mine))[:, :K]
    ref["xd"][...] = step[1]
    mine = ref["xd"][pl.ds(pl.multiple_of(zr * 8, 8), 8)]
    out_d[...] = jnp.where(zq == 0, mine, swap(mine))[:, :K]
    out_b[...] = pltpu.roll(step[2], lax.rem(Q - stu * 8, Q), 1)[:, :8]

    for name, first, last in sent:
        like = ref[name].at[pl.ds(first, last - first)]
        pltpu.make_async_copy(like, like, ssem.at[index_of[name]]).wait()


def buffers(dims):
    ZL, X, ZH, Y, C = (dims[n] for n in ("ZL", "X", "ZH", "Y", "C"))
    Q, YB, XB = ZL * X * 8, C * 8, ZL // 2 * 8
    shapes = {
        "t1": (ZH * C, 8, W), "d1": (ZL, 8, W), "b1": (ZL, 1, Q),
        "t2": (Y, YB, W), "d2": (X, XB, W), "b2": (X, 1, Q),
    }
    for tag, n in (("1", 2), ("2", 1)):
        shapes["ra" + tag] = (Y, n * YB, W)
        shapes["rb" + tag] = (Y - 1, n * YB, W)
        shapes["rc" + tag] = (ZH * C, n * YB, W)
        shapes["ca" + tag] = (X, n * XB, W)
        shapes["cb" + tag] = (X - 1, n * XB, W)
        shapes["cc" + tag] = (ZL, n * XB, W)
        shapes["sa" + tag] = (X, n, Q)
        shapes["sb" + tag] = (ZL, n, Q)
        shapes["rg" + tag] = (Y, YB, W)
        shapes["cg" + tag] = (X, XB, W)
    for tag, n in (("1", 2), ("2", 1), ("3", 1)):
        shapes["p" + tag] = (X * Y, n, W)
        shapes["q" + tag] = (ZL * ZH * C, n, W)
    shapes["xt"] = (YB, W)
    shapes["xd"] = (XB, W)
    return shapes


def shards(dims, codes, theta, disc, intercept):
    shapes = buffers(dims)
    names = tuple(shapes)
    vmem = pl.BlockSpec(memory_space=pltpu.VMEM)
    outs = pl.pallas_call(
        functools.partial(kernel, dims, names),
        out_shape=(
            jax.ShapeDtypeStruct(theta.shape, F32),
            jax.ShapeDtypeStruct(disc.shape, F32),
            jax.ShapeDtypeStruct((1, intercept.shape[0]), F32),
        ),
        in_specs=[pl.BlockSpec(memory_space=pl.ANY), vmem, vmem, pl.BlockSpec(memory_space=pltpu.SMEM)],
        out_specs=(vmem, vmem, vmem),
        scratch_shapes=[pltpu.VMEM(codes.shape, jnp.int32)]
        + [pltpu.VMEM(shape, F32) for shape in shapes.values()]
        + [
            pltpu.SemaphoreType.DMA((len(names),)),
            pltpu.SemaphoreType.DMA((len(names),)),
            pltpu.SemaphoreType.DMA,
        ],
        compiler_params=pltpu.CompilerParams(collective_id=0, has_side_effects=True),
    )(codes, theta, disc, intercept)
    return outs[0], outs[1], outs[2].reshape(intercept.shape)


def solution(mesh):
    return jax.shard_map(
        functools.partial(shards, DIMS),
        mesh=mesh,
        in_specs=(P("stu", "que"), P(("stu", "que"), None), P(("que", "stu"), None), P(("que", "stu"))),
        out_specs=(P(("stu", "que"), None), P(("que", "stu"), None), P(("que", "stu"))),
        check_vma=False,
    )
```

```python
import functools

import jax
import jax.numpy as jnp
from jax import lax
from jax.experimental import pallas as pl
from jax.experimental.pallas import tpu as pltpu
from jax.sharding import PartitionSpec as P

DIMS = dict(ZL=4, X=4, ZH=2, Y=8, C=2)
K = 64
W = 128
MESH = pl.DeviceIdType.MESH
F32 = jnp.float32
HIGH = lax.Precision.HIGHEST


def dot_nn(a, b):
    return lax.dot_general(a, b, (((1,), (0,)), ((), ())), precision=HIGH, preferred_element_type=F32)


def dot_nt(a, b):
    return lax.dot_general(a, b, (((1,), (1,)), ((), ())), precision=HIGH, preferred_element_type=F32)


def dot_tn(a, b):
    return lax.dot_general(a, b, (((0,), (0,)), ((), ())), precision=HIGH, preferred_element_type=F32)


def tree_sum(parts):
    parts = list(parts)
    while len(parts) > 1:
        parts = [parts[i] + parts[i + 1] if i + 1 < len(parts) else parts[i] for i in range(0, len(parts), 2)]
    return parts[0]


def far_first(count):
    return sorted(range(1, count), key=lambda k: ({4: 0, 5: 1, 3: 2, 7: 3, 6: 4, 2: 5, 1: 6}.get(k % 8, 7), -k))


def kernel(dims, names, codes_hbm, theta_hbm, disc_hbm, icpt_hbm, out_t, out_d, out_b, *rest):
    ZL, X, ZH, Y, C = (dims[n] for n in ("ZL", "X", "ZH", "Y", "C"))
    ref = dict(zip(names, rest))
    codes_v, theta_v, disc_v, icpt_s, made_t, made_d, made_b, ssem, rsem, lsem = rest[len(names):]
    stu, que = lax.axis_index("stu"), lax.axis_index("que")
    zl, x = stu // X, stu % X
    zh, y, core = que // (Y * C), (que // C) % Y, que % C
    half = ZL // 2
    zq, zr = zl // half, zl % half
    Q = ZL * X * 8
    YB, XB = C * 8, half * 8
    SH = Y * YB
    NXY, NZC = X * Y, ZL * ZH * C

    def at(zl_, x_, zh_, y_, core_):
        return (zl_ * X + x_, (zh_ * Y + y_) * C + core_)

    def dev_y(k):
        return at(zl, x, zh, jnp.bitwise_xor(y, k), core)

    def dev_x(k):
        return at(zl, jnp.bitwise_xor(x, k), zh, y, core)

    def dev_hc(k):
        return at(zl, x, jnp.bitwise_xor(zh, k // C), y, jnp.bitwise_xor(core, k % C))

    def dev_l(k):
        return at(jnp.bitwise_xor(zl, k), x, zh, y, core)

    def dev_xy(k):
        return at(zl, jnp.bitwise_xor(x, k // Y), zh, jnp.bitwise_xor(y, k % Y), core)

    def dev_zc(k):
        return at(
            jnp.bitwise_xor(zl, k // (ZH * C)), x, jnp.bitwise_xor(zh, (k // C) % ZH), y, jnp.bitwise_xor(core, k % C)
        )

    index_of = {n: i for i, n in enumerate(names)}
    sent = []

    def send(src, name, slot, device):
        pltpu.make_async_remote_copy(
            src_ref=src,
            dst_ref=ref[name].at[slot],
            send_sem=ssem.at[index_of[name]],
            recv_sem=rsem.at[index_of[name]],
            device_id=device,
            device_id_type=MESH,
        ).start()

    def spread(name, count, dev):
        for k in far_first(count):
            send(ref[name].at[0], name, k, dev(k))
        sent.append((name, 1, count))

    def scatter(src, name, count, me, dev):
        for k in far_first(count):
            send(ref[src].at[jnp.bitwise_xor(me, k)], name, k - 1, dev(k))
        sent.append((name, 0, count - 1))

    def arrived(name, lo, hi):
        r = ref[name].at[pl.ds(lo, hi - lo)]
        pltpu.make_async_copy(r, r, rsem.at[index_of[name]]).wait()

    def total(name, count):
        return tree_sum(ref[name][k] for k in range(count))

    fetches = [
        pltpu.make_async_copy(src, dst, lsem.at[i])
        for i, (src, dst) in enumerate(
            ((theta_hbm, theta_v), (disc_hbm, disc_v), (icpt_hbm, icpt_s), (codes_hbm, codes_v))
        )
    ]
    for fetch in fetches[:3]:
        fetch.start()

    barrier = pltpu.get_barrier_semaphore()
    partners = [dev_y(k) for k in far_first(Y)] + [dev_hc(k) for k in far_first(ZH * C)]
    partners += [dev_l(k) for k in far_first(ZL)] + [dev_x(k) for k in far_first(X)]
    for partner in partners:
        pl.semaphore_signal(barrier, inc=1, device_id=partner, device_id_type=MESH)
    fetches[3].start()

    low8 = lax.broadcasted_iota(jnp.int32, (8, W), 1) // K
    fetches[0].wait()
    th = theta_v[...]
    ref["t1"][0] = jnp.where(low8 == zh, jnp.concatenate([th, th], 1), 0.0)
    fetches[1].wait()
    dc = disc_v[...]
    ref["d1"][0] = jnp.where(low8 == zq, jnp.concatenate([dc, dc], 1), 0.0)
    fetches[2].wait()
    qlane = lax.broadcasted_iota(jnp.int32, (1, Q), 1)
    brow = jnp.zeros((1, Q), F32)
    for k in range(8):
        brow = jnp.where(qlane == stu * 8 + k, icpt_s[k], brow)
    ref["b1"][0] = brow

    pl.semaphore_wait(barrier, len(partners))

    spread("t1", ZH * C, dev_hc)
    spread("d1", ZL, dev_l)
    spread("b1", ZL, dev_l)

    arrived("d1", 1, ZL)
    slot_l = lambda z: jnp.bitwise_xor(zl, z)
    d_own = jnp.concatenate([ref["d1"][slot_l(r)] + ref["d1"][slot_l(half + r)] for r in range(half)], 0)
    ref["d2"][0] = d_own
    spread("d2", X, dev_x)
    arrived("b1", 1, ZL)
    ref["b2"][0] = total("b1", ZL)
    spread("b2", X, dev_x)
    arrived("t1", 1, ZH * C)
    slot_hc = lambda h, c: jnp.bitwise_xor(zh, h) * C + jnp.bitwise_xor(core, c)
    t_own = jnp.concatenate([ref["t1"][slot_hc(0, c)] + ref["t1"][slot_hc(1, c)] for c in range(C)], 0)
    ref["t2"][0] = t_own
    spread("t2", Y, dev_y)

    def rows_of(name):
        return jnp.concatenate([ref[name][jnp.bitwise_xor(y, k)] for k in range(Y)], 0)

    def low(v):
        return lax.broadcasted_iota(jnp.int32, v.shape, 1) < K

    def swap(v):
        return pltpu.roll(v, K, 1)

    def cols_of(name):
        packed = jnp.concatenate(
            [ref[name][jnp.bitwise_xor(x, k), pl.ds(r * 8, 8)] for r in range(half) for k in range(X)], 0
        )
        turned = swap(packed)
        lo = low(packed)
        zero = jnp.zeros_like(packed)
        first = jnp.concatenate([jnp.where(lo, packed, zero), jnp.where(lo, turned, zero)], 0)
        second = jnp.concatenate([jnp.where(lo, zero, turned), jnp.where(lo, zero, packed)], 0)
        return first, second

    def pack_cols(v):
        upper, lower = v[: Q // 2], v[Q // 2 :]
        return jnp.where(low(upper), upper, lower)

    arrived("d2", 1, X)
    dd = cols_of("d2")
    arrived("b2", 1, X)
    bias = total("b2", X)
    fetches[3].wait()
    arrived("t2", 1, Y)
    theta = rows_of("t2")
    turned = swap(theta)
    lo = low(theta)
    tt = (jnp.where(lo, theta, turned), jnp.where(lo, turned, theta))

    resid, weight = [], []
    for h in range(ZH):
        prob = jax.nn.sigmoid(dot_nt(theta, dd[h]) + bias)
        code = codes_v[pl.ds(h * SH, SH)]
        observed = (code > 0).astype(F32)
        correct = (code == 2).astype(F32)
        resid.append(observed * (prob - correct))
        weight.append(observed * prob * (1.0 - prob))

    def row_part(u, d):
        return dot_nn(u[0], d[0]) + dot_nn(u[1], d[1])

    def col_part(u, t):
        return pack_cols(dot_tn(u[0], t[0]) + dot_tn(u[1], t[1]))

    def col_sum(u):
        return jnp.sum(u[0], 0, keepdims=True) + jnp.sum(u[1], 0, keepdims=True)

    def put_rows(name, offset, v):
        for k in range(Y):
            ref[name][k, pl.ds(offset, YB)] = v[k * YB : (k + 1) * YB]

    def put_cols(name, offset, v):
        for k in range(X):
            for r in range(half):
                start = (r * X + k) * 8
                ref[name][k, pl.ds(offset + r * 8, 8)] = v[start : start + 8]

    def reduce_all(tag, row_list, col_list, sums, between=None):
        for i, v in enumerate(row_list):
            put_rows("ra" + tag, i * YB, v)
        scatter("ra" + tag, "rb" + tag, Y, y, dev_y)
        for i, v in enumerate(col_list):
            put_cols("ca" + tag, i * XB, v)
        scatter("ca" + tag, "cb" + tag, X, x, dev_x)
        ref["sa" + tag][0] = sums
        spread("sa" + tag, X, dev_x)
        arrived("cb" + tag, 0, X - 1)
        ref["cc" + tag][0] = tree_sum([ref["ca" + tag][x]] + [ref["cb" + tag][k] for k in range(X - 1)])
        spread("cc" + tag, ZL, dev_l)
        arrived("sa" + tag, 1, X)
        ref["sb" + tag][0] = total("sa" + tag, X)
        spread("sb" + tag, ZL, dev_l)
        if between is not None:
            between()
        arrived("rb" + tag, 0, Y - 1)
        ref["rc" + tag][0] = tree_sum([ref["ra" + tag][y]] + [ref["rb" + tag][k] for k in range(Y - 1)])
        spread("rc" + tag, ZH * C, dev_hc)
        arrived("cc" + tag, 1, ZL)
        cols = total("cc" + tag, ZL)
        arrived("sb" + tag, 1, ZL)
        sums = total("sb" + tag, ZL)
        arrived("rc" + tag, 1, ZH * C)
        rows = total("rc" + tag, ZH * C)
        return rows, cols, sums

    def gather_start(tag, rows, cols):
        ref["rg" + tag][0] = rows
        spread("rg" + tag, Y, dev_y)
        ref["cg" + tag][0] = cols
        spread("cg" + tag, X, dev_x)

    def change_of(tag, vb):
        arrived("cg" + tag, 1, X)
        va = cols_of("cg" + tag)
        arrived("rg" + tag, 1, Y)
        left = jnp.concatenate([rows_of("rg" + tag), theta], 1)
        return [dot_nt(left, jnp.concatenate([dd[h], va[h]], 1)) + vb for h in range(ZH)]

    def lanes(v):
        s = jnp.sum(v, 0, keepdims=True)
        if s.shape[1] < W:
            s = jnp.concatenate([s, jnp.zeros((1, W - s.shape[1]), F32)], 1)
        return s

    def inner(u, v):
        rows = lanes(u[0] * v[0]) * (1.0 / (ZH * C))
        cols = lanes(u[1] * v[1]) * (1.0 / ZL)
        return rows + cols + lanes(u[2] * v[2]) * (1.0 / (ZL * X))

    def first_round(tag, values):
        for i, v in enumerate(values):
            ref["p" + tag][0, pl.ds(i, 1)] = v
        spread("p" + tag, NXY, dev_xy)

    def second_round(tag):
        arrived("p" + tag, 1, NXY)
        ref["q" + tag][0] = jnp.sum(ref["p" + tag][...], 0)
        spread("q" + tag, NZC, dev_zc)

    def last_round(tag):
        arrived("q" + tag, 1, NZC)
        return jnp.sum(jnp.sum(ref["q" + tag][...], 0), 1, keepdims=True)

    d2 = [d * d for d in dd]
    t2 = [t * t for t in tt]
    sums = jnp.concatenate([col_sum(resid), col_sum(weight)], 0)
    rows, cols, sums = reduce_all(
        "1",
        (row_part(resid, dd), row_part(weight, d2)),
        (col_part(resid, tt), col_part(weight, t2)),
        sums,
    )
    r = (-(rows[:YB] + t_own), -(cols[:XB] + d_own), -(sums[0:1] + bias))
    dg = (rows[YB:] + 1.0, cols[XB:] + 1.0, sums[1:2] + 1.0)
    z = [a / b for a, b in zip(r, dg)]
    gather_start("1", z[0], z[1])
    rz_part = inner(r, z)
    zz_part = inner(z, z)
    change = change_of("1", z[2])
    scaled = [w * c for w, c in zip(weight, change)]
    pq_part = lanes(scaled[0] * change[0]) + lanes(scaled[1] * change[1]) + zz_part
    first_round("1", (rz_part, pq_part))
    rows, cols, sums = reduce_all(
        "2",
        (row_part(scaled, dd),),
        (col_part(scaled, tt),),
        col_sum(scaled),
        between=lambda: second_round("1"),
    )
    image = (rows + z[0], cols + z[1], sums + z[2])
    scalars = last_round("1")
    rz, pq = scalars[0:1], scalars[1:2]
    alpha = rz / pq
    r = [a - alpha * b for a, b in zip(r, image)]
    z_next = [a / b for a, b in zip(r, dg)]
    gather_start("2", z_next[0], z_next[1])
    new_part = inner(r, z_next)
    own_part, cross_part = inner(z_next, z_next), inner(z_next, z)
    change_next = change_of("2", z_next[2])
    for w, c, n in zip(weight, change, change_next):
        wn = w * n
        own_part = own_part + lanes(wn * n)
        cross_part = cross_part + lanes(wn * c)
    first_round("2", (new_part, own_part, cross_part))
    second_round("2")
    scalars = last_round("2")
    new, own, cross = scalars[0:1], scalars[1:2], scalars[2:3]
    beta = new / rz
    alpha_two = new / (own + 2.0 * beta * cross + beta * beta * pq)
    step = [
        (alpha * a + alpha_two * (b + beta * a)) * jnp.sqrt(d) for a, b, d in zip(z, z_next, dg)
    ]

    ref["xt"][...] = step[0]
    mine = ref["xt"][pl.ds(pl.multiple_of(core * 8, 8), 8)]
    made_t[...] = jnp.where(zh == 0, mine, swap(mine))[:, :K]
    ref["xd"][...] = step[1]
    mine = ref["xd"][pl.ds(pl.multiple_of(zr * 8, 8), 8)]
    made_d[...] = jnp.where(zq == 0, mine, swap(mine))[:, :K]
    made_b[...] = pltpu.roll(step[2], lax.rem(Q - stu * 8, Q), 1)[:, :8]
    stores = [
        pltpu.make_async_copy(src, dst, lsem.at[4 + i])
        for i, (src, dst) in enumerate(((made_t, out_t), (made_d, out_d), (made_b, out_b)))
    ]
    for store in stores:
        store.start()

    for name, first, last in sent:
        like = ref[name].at[pl.ds(first, last - first)]
        pltpu.make_async_copy(like, like, ssem.at[index_of[name]]).wait()
    for store in stores:
        store.wait()


def hand_over(*refs):
    ins, outs, held, sems = refs[:3], refs[3:6], refs[6:9], refs[9]
    first = [pltpu.make_async_copy(a, b, sems.at[i]) for i, (a, b) in enumerate(zip(ins, held))]
    second = [pltpu.make_async_copy(a, b, sems.at[3 + i]) for i, (a, b) in enumerate(zip(held, outs))]
    for copy in first:
        copy.start()
    for a, b in zip(first, second):
        a.wait()
        b.start()
    for copy in second:
        copy.wait()


def buffers(dims):
    ZL, X, ZH, Y, C = (dims[n] for n in ("ZL", "X", "ZH", "Y", "C"))
    Q, YB, XB = ZL * X * 8, C * 8, ZL // 2 * 8
    shapes = {
        "t1": (ZH * C, 8, W), "d1": (ZL, 8, W), "b1": (ZL, 1, Q),
        "t2": (Y, YB, W), "d2": (X, XB, W), "b2": (X, 1, Q),
    }
    for tag, n in (("1", 2), ("2", 1)):
        shapes["ra" + tag] = (Y, n * YB, W)
        shapes["rb" + tag] = (Y - 1, n * YB, W)
        shapes["rc" + tag] = (ZH * C, n * YB, W)
        shapes["ca" + tag] = (X, n * XB, W)
        shapes["cb" + tag] = (X - 1, n * XB, W)
        shapes["cc" + tag] = (ZL, n * XB, W)
        shapes["sa" + tag] = (X, n, Q)
        shapes["sb" + tag] = (ZL, n, Q)
        shapes["rg" + tag] = (Y, YB, W)
        shapes["cg" + tag] = (X, XB, W)
    for tag, n in (("1", 2), ("2", 3)):
        shapes["p" + tag] = (X * Y, n, W)
        shapes["q" + tag] = (ZL * ZH * C, n, W)
    shapes["xt"] = (YB, W)
    shapes["xd"] = (XB, W)
    return shapes


def shards(dims, codes, theta, disc, intercept):
    shapes = buffers(dims)
    names = tuple(shapes)
    made = (
        jax.ShapeDtypeStruct(theta.shape, F32),
        jax.ShapeDtypeStruct(disc.shape, F32),
        jax.ShapeDtypeStruct((1, intercept.shape[0]), F32),
    )
    hbm = pl.BlockSpec(memory_space=pltpu.HBM)
    outs = pl.pallas_call(
        functools.partial(kernel, dims, names),
        out_shape=made,
        in_specs=[hbm, hbm, hbm, hbm],
        out_specs=(hbm, hbm, hbm),
        scratch_shapes=[pltpu.VMEM(shape, F32) for shape in shapes.values()]
        + [
            pltpu.VMEM(codes.shape, jnp.int32),
            pltpu.VMEM(theta.shape, F32),
            pltpu.VMEM(disc.shape, F32),
            pltpu.SMEM(intercept.shape, F32),
        ]
        + [pltpu.VMEM(s.shape, F32) for s in made]
        + [
            pltpu.SemaphoreType.DMA((len(names),)),
            pltpu.SemaphoreType.DMA((len(names),)),
            pltpu.SemaphoreType.DMA((7,)),
        ],
        compiler_params=pltpu.CompilerParams(collective_id=0, has_side_effects=True),
    )(codes, theta, disc, intercept)
    outs = pl.pallas_call(
        hand_over,
        out_shape=made,
        in_specs=[hbm, hbm, hbm],
        out_specs=(hbm, hbm, hbm),
        scratch_shapes=[pltpu.VMEM(s.shape, F32) for s in made] + [pltpu.SemaphoreType.DMA((6,))],
    )(*outs)
    return outs[0], outs[1], outs[2].reshape(intercept.shape)


def solution(mesh):
    return jax.shard_map(
        functools.partial(shards, DIMS),
        mesh=mesh,
        in_specs=(P("stu", "que"), P(("stu", "que"), None), P(("que", "stu"), None), P(("que", "stu"))),
        out_specs=(P(("stu", "que"), None), P(("que", "stu"), None), P(("que", "stu"))),
        check_vma=False,
    )
```

```python
import functools

import jax
import jax.numpy as jnp
from jax import lax
from jax.experimental import pallas as pl
from jax.experimental.pallas import tpu as pltpu
from jax.sharding import PartitionSpec as P

DIMS = dict(ZL=4, X=4, ZH=2, Y=8, C=2)
K = 64
W = 128
MESH = pl.DeviceIdType.MESH
F32 = jnp.float32


def split(v):
    head = v.astype(jnp.bfloat16)
    return head, (v - head.astype(F32)).astype(jnp.bfloat16)


def dot(a, b, ca, cb):
    def one(u, v):
        return lax.dot_general(u, v, (((ca,), (cb,)), ((), ())), preferred_element_type=F32)
    return one(a[0], b[0]) + (one(a[0], b[1]) + one(a[1], b[0]))


def dot_nn(a, b):
    return dot(a, b, 1, 0)


def dot_nt(a, b):
    return dot(a, b, 1, 1)


def dot_tn(a, b):
    return dot(a, b, 0, 0)


def beside(a, b):
    return tuple(jnp.concatenate([u, v], 1) for u, v in zip(a, b))


def tree_sum(parts):
    parts = list(parts)
    while len(parts) > 1:
        parts = [parts[i] + parts[i + 1] if i + 1 < len(parts) else parts[i] for i in range(0, len(parts), 2)]
    return parts[0]


def far_first(count):
    return sorted(range(1, count), key=lambda k: ({4: 0, 5: 1, 3: 2, 7: 3, 6: 4, 2: 5, 1: 6}.get(k % 8, 7), -k))


def kernel(dims, names, codes_hbm, theta_hbm, disc_hbm, icpt_hbm, out_t, out_d, out_b, *rest):
    ZL, X, ZH, Y, C = (dims[n] for n in ("ZL", "X", "ZH", "Y", "C"))
    ref = dict(zip(names, rest))
    codes_v, theta_v, disc_v, icpt_s, ssem, rsem, lsem = rest[len(names):]
    stu, que = lax.axis_index("stu"), lax.axis_index("que")
    zl, x = stu // X, stu % X
    zh, y, core = que // (Y * C), (que // C) % Y, que % C
    half = ZL // 2
    zq, zr = zl // half, zl % half
    Q = ZL * X * 8
    YB, XB = C * 8, half * 8
    SH = Y * YB
    NXY, NZC = X * Y, ZL * ZH * C

    def at(zl_, x_, zh_, y_, core_):
        return (zl_ * X + x_, (zh_ * Y + y_) * C + core_)

    def dev_y(k):
        return at(zl, x, zh, jnp.bitwise_xor(y, k), core)

    def dev_x(k):
        return at(zl, jnp.bitwise_xor(x, k), zh, y, core)

    def dev_hc(k):
        return at(zl, x, jnp.bitwise_xor(zh, k // C), y, jnp.bitwise_xor(core, k % C))

    def dev_l(k):
        return at(jnp.bitwise_xor(zl, k), x, zh, y, core)

    def dev_xy(k):
        return at(zl, jnp.bitwise_xor(x, k // Y), zh, jnp.bitwise_xor(y, k % Y), core)

    def dev_zc(k):
        return at(
            jnp.bitwise_xor(zl, k // (ZH * C)), x, jnp.bitwise_xor(zh, (k // C) % ZH), y, jnp.bitwise_xor(core, k % C)
        )

    index_of = {n: i for i, n in enumerate(names)}
    sent = []

    def send(src, name, slot, device):
        pltpu.make_async_remote_copy(
            src_ref=src,
            dst_ref=ref[name].at[slot],
            send_sem=ssem.at[index_of[name]],
            recv_sem=rsem.at[index_of[name]],
            device_id=device,
            device_id_type=MESH,
        ).start()

    def spread(name, count, dev):
        for k in far_first(count):
            send(ref[name].at[0], name, k, dev(k))
        sent.append((name, 1, count))

    def scatter(src, name, count, me, dev):
        for k in far_first(count):
            send(ref[src].at[jnp.bitwise_xor(me, k)], name, k - 1, dev(k))
        sent.append((name, 0, count - 1))

    def arrived(name, lo, hi):
        r = ref[name].at[pl.ds(lo, hi - lo)]
        pltpu.make_async_copy(r, r, rsem.at[index_of[name]]).wait()

    def total(name, count):
        return tree_sum(ref[name][k] for k in range(count))

    fetches = [
        pltpu.make_async_copy(src, dst, lsem.at[i])
        for i, (src, dst) in enumerate(
            ((theta_hbm, theta_v), (disc_hbm, disc_v), (icpt_hbm, icpt_s), (codes_hbm, codes_v))
        )
    ]
    for fetch in fetches[:3]:
        fetch.start()

    barrier = pltpu.get_barrier_semaphore()
    partners = [dev_y(k) for k in far_first(Y)] + [dev_hc(k) for k in far_first(ZH * C)]
    partners += [dev_l(k) for k in far_first(ZL)] + [dev_x(k) for k in far_first(X)]
    for partner in partners:
        pl.semaphore_signal(barrier, inc=1, device_id=partner, device_id_type=MESH)
    fetches[3].start()

    low8 = lax.broadcasted_iota(jnp.int32, (8, W), 1) // K
    fetches[0].wait()
    th = theta_v[...]
    ref["t1"][0] = jnp.where(low8 == zh, jnp.concatenate([th, th], 1), 0.0)
    fetches[1].wait()
    dc = disc_v[...]
    ref["d1"][0] = jnp.where(low8 == zq, jnp.concatenate([dc, dc], 1), 0.0)
    fetches[2].wait()
    qlane = lax.broadcasted_iota(jnp.int32, (1, Q), 1)
    brow = jnp.zeros((1, Q), F32)
    for k in range(8):
        brow = jnp.where(qlane == stu * 8 + k, icpt_s[k], brow)
    ref["b1"][0] = brow

    pl.semaphore_wait(barrier, len(partners))

    spread("t1", ZH * C, dev_hc)
    spread("d1", ZL, dev_l)
    spread("b1", ZL, dev_l)

    arrived("d1", 1, ZL)
    slot_l = lambda z: jnp.bitwise_xor(zl, z)
    d_own = jnp.concatenate([ref["d1"][slot_l(r)] + ref["d1"][slot_l(half + r)] for r in range(half)], 0)
    ref["d2"][0] = d_own
    spread("d2", X, dev_x)
    arrived("b1", 1, ZL)
    ref["b2"][0] = total("b1", ZL)
    spread("b2", X, dev_x)
    arrived("t1", 1, ZH * C)
    slot_hc = lambda h, c: jnp.bitwise_xor(zh, h) * C + jnp.bitwise_xor(core, c)
    t_own = jnp.concatenate([ref["t1"][slot_hc(0, c)] + ref["t1"][slot_hc(1, c)] for c in range(C)], 0)
    ref["t2"][0] = t_own
    spread("t2", Y, dev_y)

    def rows_of(name):
        return jnp.concatenate([ref[name][jnp.bitwise_xor(y, k)] for k in range(Y)], 0)

    def low(v):
        return lax.broadcasted_iota(jnp.int32, v.shape, 1) < K

    def swap(v):
        return pltpu.roll(v, K, 1)

    def cols_of(name):
        packed = jnp.concatenate(
            [ref[name][jnp.bitwise_xor(x, k), pl.ds(r * 8, 8)] for r in range(half) for k in range(X)], 0
        )
        turned = swap(packed)
        lo = low(packed)
        zero = jnp.zeros_like(packed)
        first = jnp.concatenate([jnp.where(lo, packed, zero), jnp.where(lo, turned, zero)], 0)
        second = jnp.concatenate([jnp.where(lo, zero, turned), jnp.where(lo, zero, packed)], 0)
        return first, second

    def pack_cols(v):
        upper, lower = v[: Q // 2], v[Q // 2 :]
        return jnp.where(low(upper), upper, lower)

    arrived("d2", 1, X)
    dd = cols_of("d2")
    arrived("b2", 1, X)
    bias = total("b2", X)
    fetches[3].wait()
    arrived("t2", 1, Y)
    theta = rows_of("t2")
    turned = swap(theta)
    lo = low(theta)
    tt = (jnp.where(lo, theta, turned), jnp.where(lo, turned, theta))

    theta_s, dd_s, tt_s = split(theta), [split(d) for d in dd], [split(t) for t in tt]

    resid, weight = [], []
    for h in range(ZH):
        prob = jax.nn.sigmoid(dot_nt(theta_s, dd_s[h]) + bias)
        code = codes_v[pl.ds(h * SH, SH)]
        observed = (code > 0).astype(F32)
        correct = (code == 2).astype(F32)
        resid.append(observed * (prob - correct))
        weight.append(observed * prob * (1.0 - prob))

    def row_part(u, d):
        return dot_nn(u[0], d[0]) + dot_nn(u[1], d[1])

    def col_part(u, t):
        return pack_cols(dot_tn(u[0], t[0]) + dot_tn(u[1], t[1]))

    def col_sum(u):
        return jnp.sum(u[0], 0, keepdims=True) + jnp.sum(u[1], 0, keepdims=True)

    def put_rows(name, offset, v):
        for k in range(Y):
            ref[name][k, pl.ds(offset, YB)] = v[k * YB : (k + 1) * YB]

    def put_cols(name, offset, v):
        for k in range(X):
            for r in range(half):
                start = (r * X + k) * 8
                ref[name][k, pl.ds(offset + r * 8, 8)] = v[start : start + 8]

    def reduce_all(tag, row_list, col_list, sums, between=None):
        for i, v in enumerate(row_list):
            put_rows("ra" + tag, i * YB, v)
        scatter("ra" + tag, "rb" + tag, Y, y, dev_y)
        for i, v in enumerate(col_list):
            put_cols("ca" + tag, i * XB, v)
        scatter("ca" + tag, "cb" + tag, X, x, dev_x)
        ref["sa" + tag][0] = sums
        spread("sa" + tag, X, dev_x)
        arrived("cb" + tag, 0, X - 1)
        ref["cc" + tag][0] = tree_sum([ref["ca" + tag][x]] + [ref["cb" + tag][k] for k in range(X - 1)])
        spread("cc" + tag, ZL, dev_l)
        arrived("sa" + tag, 1, X)
        ref["sb" + tag][0] = total("sa" + tag, X)
        spread("sb" + tag, ZL, dev_l)
        arrived("rb" + tag, 0, Y - 1)
        ref["rc" + tag][0] = tree_sum([ref["ra" + tag][y]] + [ref["rb" + tag][k] for k in range(Y - 1)])
        spread("rc" + tag, ZH * C, dev_hc)
        if between is not None:
            between()
        arrived("cc" + tag, 1, ZL)
        cols = total("cc" + tag, ZL)
        arrived("sb" + tag, 1, ZL)
        sums = total("sb" + tag, ZL)
        arrived("rc" + tag, 1, ZH * C)
        rows = total("rc" + tag, ZH * C)
        return rows, cols, sums

    def gather_start(tag, rows, cols):
        ref["rg" + tag][0] = rows
        spread("rg" + tag, Y, dev_y)
        ref["cg" + tag][0] = cols
        spread("cg" + tag, X, dev_x)

    def change_of(tag, vb):
        arrived("cg" + tag, 1, X)
        va = cols_of("cg" + tag)
        arrived("rg" + tag, 1, Y)
        left = beside(split(rows_of("rg" + tag)), theta_s)
        return [dot_nt(left, beside(dd_s[h], split(va[h]))) + vb for h in range(ZH)]

    def lanes(v):
        s = jnp.sum(v, 0, keepdims=True)
        if s.shape[1] < W:
            s = jnp.concatenate([s, jnp.zeros((1, W - s.shape[1]), F32)], 1)
        return s

    def inner(u, v):
        rows = lanes(u[0] * v[0]) * (1.0 / (ZH * C))
        cols = lanes(u[1] * v[1]) * (1.0 / ZL)
        return rows + cols + lanes(u[2] * v[2]) * (1.0 / (ZL * X))

    def first_round(tag, values):
        for i, v in enumerate(values):
            ref["p" + tag][0, pl.ds(i, 1)] = v
        spread("p" + tag, NXY, dev_xy)

    def second_round(tag):
        arrived("p" + tag, 1, NXY)
        ref["q" + tag][0] = jnp.sum(ref["p" + tag][...], 0)
        spread("q" + tag, NZC, dev_zc)

    def last_round(tag):
        arrived("q" + tag, 1, NZC)
        return jnp.sum(jnp.sum(ref["q" + tag][...], 0), 1, keepdims=True)

    d2 = [split(d * d) for d in dd]
    t2 = [split(t * t) for t in tt]
    resid_s, weight_s = [split(u) for u in resid], [split(u) for u in weight]
    sums = jnp.concatenate([col_sum(resid), col_sum(weight)], 0)
    rows, cols, sums = reduce_all(
        "1",
        (row_part(resid_s, dd_s), row_part(weight_s, d2)),
        (col_part(resid_s, tt_s), col_part(weight_s, t2)),
        sums,
    )
    r = (-(rows[:YB] + t_own), -(cols[:XB] + d_own), -(sums[0:1] + bias))
    dg = (rows[YB:] + 1.0, cols[XB:] + 1.0, sums[1:2] + 1.0)
    z = [a / b for a, b in zip(r, dg)]
    gather_start("1", z[0], z[1])
    rz_part = inner(r, z)
    zz_part = inner(z, z)
    change = change_of("1", z[2])
    scaled = [w * c for w, c in zip(weight, change)]
    scaled_s = [split(u) for u in scaled]
    pq_part = lanes(scaled[0] * change[0]) + lanes(scaled[1] * change[1]) + zz_part
    first_round("1", (rz_part, pq_part))
    rows, cols, sums = reduce_all(
        "2",
        (row_part(scaled_s, dd_s),),
        (col_part(scaled_s, tt_s),),
        col_sum(scaled),
        between=lambda: second_round("1"),
    )
    image = (rows + z[0], cols + z[1], sums + z[2])
    scaled_image = [a / b for a, b in zip(image, dg)]
    gather_start("2", scaled_image[0], scaled_image[1])
    scalars = last_round("1")
    rz, pq = scalars[0:1], scalars[1:2]
    alpha = rz / pq
    r = [a - alpha * b for a, b in zip(r, image)]
    z_next = [a / b for a, b in zip(r, dg)]
    new_part = inner(r, z_next)
    own_part, cross_part = inner(z_next, z_next), inner(z_next, z)
    for w, c, s in zip(weight, change, change_of("2", scaled_image[2])):
        n = c - alpha * s
        wn = w * n
        own_part = own_part + lanes(wn * n)
        cross_part = cross_part + lanes(wn * c)
    first_round("2", (new_part, own_part, cross_part))
    second_round("2")
    scalars = last_round("2")
    new, own, cross = scalars[0:1], scalars[1:2], scalars[2:3]
    beta = new / rz
    alpha_two = new / (own + 2.0 * beta * cross + beta * beta * pq)
    step = [
        (alpha * a + alpha_two * (b + beta * a)) * jnp.sqrt(d) for a, b, d in zip(z, z_next, dg)
    ]

    ref["xt"][...] = step[0]
    mine = ref["xt"][pl.ds(pl.multiple_of(core * 8, 8), 8)]
    out_t[...] = jnp.where(zh == 0, mine, swap(mine))[:, :K]
    ref["xd"][...] = step[1]
    mine = ref["xd"][pl.ds(pl.multiple_of(zr * 8, 8), 8)]
    out_d[...] = jnp.where(zq == 0, mine, swap(mine))[:, :K]
    out_b[...] = pltpu.roll(step[2], lax.rem(Q - stu * 8, Q), 1)[:, :8]

    for name, first, last in sent:
        like = ref[name].at[pl.ds(first, last - first)]
        pltpu.make_async_copy(like, like, ssem.at[index_of[name]]).wait()


def hand_over(*refs):
    ins, outs, sems = refs[:3], refs[3:6], refs[6]
    copies = [pltpu.make_async_copy(a, b, sems.at[i]) for i, (a, b) in enumerate(zip(ins, outs))]
    for copy in copies:
        copy.start()
    for copy in copies:
        copy.wait()


def buffers(dims):
    ZL, X, ZH, Y, C = (dims[n] for n in ("ZL", "X", "ZH", "Y", "C"))
    Q, YB, XB = ZL * X * 8, C * 8, ZL // 2 * 8
    shapes = {
        "t1": (ZH * C, 8, W), "d1": (ZL, 8, W), "b1": (ZL, 1, Q),
        "t2": (Y, YB, W), "d2": (X, XB, W), "b2": (X, 1, Q),
    }
    for tag, n in (("1", 2), ("2", 1)):
        shapes["ra" + tag] = (Y, n * YB, W)
        shapes["rb" + tag] = (Y - 1, n * YB, W)
        shapes["rc" + tag] = (ZH * C, n * YB, W)
        shapes["ca" + tag] = (X, n * XB, W)
        shapes["cb" + tag] = (X - 1, n * XB, W)
        shapes["cc" + tag] = (ZL, n * XB, W)
        shapes["sa" + tag] = (X, n, Q)
        shapes["sb" + tag] = (ZL, n, Q)
        shapes["rg" + tag] = (Y, YB, W)
        shapes["cg" + tag] = (X, XB, W)
    for tag, n in (("1", 2), ("2", 3)):
        shapes["p" + tag] = (X * Y, n, W)
        shapes["q" + tag] = (ZL * ZH * C, n, W)
    shapes["xt"] = (YB, W)
    shapes["xd"] = (XB, W)
    return shapes


def shards(dims, codes, theta, disc, intercept):
    shapes = buffers(dims)
    names = tuple(shapes)
    made = (
        jax.ShapeDtypeStruct(theta.shape, F32),
        jax.ShapeDtypeStruct(disc.shape, F32),
        jax.ShapeDtypeStruct((1, intercept.shape[0]), F32),
    )
    hbm, vmem = pl.BlockSpec(memory_space=pltpu.HBM), pl.BlockSpec(memory_space=pltpu.VMEM)
    outs = pl.pallas_call(
        functools.partial(kernel, dims, names),
        out_shape=tuple(pltpu.VMEM(s.shape, F32) for s in made),
        in_specs=[hbm, hbm, hbm, hbm],
        out_specs=(vmem, vmem, vmem),
        scratch_shapes=[pltpu.VMEM(shape, F32) for shape in shapes.values()]
        + [
            pltpu.VMEM(codes.shape, jnp.int32),
            pltpu.VMEM(theta.shape, F32),
            pltpu.VMEM(disc.shape, F32),
            pltpu.SMEM(intercept.shape, F32),
            pltpu.SemaphoreType.DMA((len(names),)),
            pltpu.SemaphoreType.DMA((len(names),)),
            pltpu.SemaphoreType.DMA((4,)),
        ],
        compiler_params=pltpu.CompilerParams(collective_id=0, has_side_effects=True, vmem_limit_bytes=32 * 2**20),
    )(*(pltpu.with_memory_space_constraint(a, pltpu.HBM) for a in (codes, theta, disc, intercept)))
    outs = pl.pallas_call(
        hand_over,
        out_shape=tuple(pltpu.HBM(s.shape, F32) for s in made),
        in_specs=[vmem, vmem, vmem],
        out_specs=(hbm, hbm, hbm),
        scratch_shapes=[pltpu.SemaphoreType.DMA((3,))],
        compiler_params=pltpu.CompilerParams(vmem_limit_bytes=2**20),
    )(*outs)
    return outs[0], outs[1], outs[2].reshape(intercept.shape)


def solution(mesh):
    return jax.shard_map(
        functools.partial(shards, DIMS),
        mesh=mesh,
        in_specs=(P("stu", "que"), P(("stu", "que"), None), P(("que", "stu"), None), P(("que", "stu"))),
        out_specs=(P(("stu", "que"), None), P(("que", "stu"), None), P(("que", "stu"))),
        check_vma=False,
    )
```

```python
import functools
import math

import jax
import jax.numpy as jnp
from jax import lax
from jax.experimental import pallas as pl
from jax.experimental.pallas import tpu as pltpu
from jax.sharding import PartitionSpec as P

DIMS = dict(ZL=4, X=4, ZH=2, Y=8, C=2)
K = 64
W = 128
LOCAL = ("ra1", "ca1", "ra2", "ca2", "xd", "sent")
SHARED = {"rb2": "rb1", "cb2": "cb1", "sa2": "sa1", "rg1": "t2", "rg2": "t2", "cg1": "d2", "cg2": "d2"}
MESH = pl.DeviceIdType.MESH
F32 = jnp.float32


def split(v):
    head = v.astype(jnp.bfloat16)
    return head, (v - head.astype(F32)).astype(jnp.bfloat16)


def dot(a, b, ca, cb):
    def one(u, v):
        return lax.dot_general(u, v, (((ca,), (cb,)), ((), ())), preferred_element_type=F32)
    return one(a[0], b[0]) + (one(a[0], b[1]) + one(a[1], b[0]))


def dot_nn(a, b):
    return dot(a, b, 1, 0)


def dot_nt(a, b):
    return dot(a, b, 1, 1)


def dot_tn(a, b):
    return dot(a, b, 0, 0)


def tree_sum(parts):
    parts = list(parts)
    while len(parts) > 1:
        parts = [parts[i] + parts[i + 1] if i + 1 < len(parts) else parts[i] for i in range(0, len(parts), 2)]
    return parts[0]


def far_first(count, unit=1):
    order = {4: 0, 5: 1, 3: 2, 7: 3, 6: 4, 2: 5, 1: 6}
    return sorted(range(1, count), key=lambda k: (order.get(k // unit % 8, 7), -k))


def kernel(dims, names, codes_hbm, theta_hbm, disc_hbm, icpt_hbm, out_t, out_d, out_b, *rest):
    ZL, X, ZH, Y, C = (dims[n] for n in ("ZL", "X", "ZH", "Y", "C"))
    ref = dict(zip(names, rest))
    codes_v, theta_v, disc_v, icpt_s, ssem, rsem, lsem = rest[len(names):]
    stu, que = lax.axis_index("stu"), lax.axis_index("que")
    zl, x = stu // X, stu % X
    zh, y, core = que // (Y * C), (que // C) % Y, que % C
    half = ZL // 2
    zq, zr = zl // half, zl % half
    Q = ZL * X * 8
    XB = half * 8
    NYC, NXY, NZC = Y * C, X * Y, ZL * ZH * C
    SH = NYC * 8
    yc = y * C + core

    def at(zl_, x_, zh_, y_, core_):
        return (zl_ * X + x_, (zh_ * Y + y_) * C + core_)

    def dev_yc(k):
        return at(zl, x, zh, jnp.bitwise_xor(y, k // C), jnp.bitwise_xor(core, k % C))

    def dev_x(k):
        return at(zl, jnp.bitwise_xor(x, k), zh, y, core)

    def dev_h(k):
        return at(zl, x, jnp.bitwise_xor(zh, k), y, core)

    def dev_l(k):
        return at(jnp.bitwise_xor(zl, k), x, zh, y, core)

    def dev_xy(k):
        return at(zl, jnp.bitwise_xor(x, k // Y), zh, jnp.bitwise_xor(y, k % Y), core)

    def dev_zc(k):
        return at(
            jnp.bitwise_xor(zl, k // (ZH * C)), x, jnp.bitwise_xor(zh, (k // C) % ZH), y, jnp.bitwise_xor(core, k % C)
        )

    serial = sorted({SHARED.get(n, n) for n in names if n not in LOCAL})
    index_of = {n: serial.index(SHARED.get(n, n)) for n in names if n not in LOCAL}
    sent = []

    def send(src, name, slot, device):
        sent.append(math.prod(src.shape))
        pltpu.make_async_remote_copy(
            src_ref=src,
            dst_ref=ref[name].at[slot],
            send_sem=ssem,
            recv_sem=rsem.at[index_of[name]],
            device_id=device,
            device_id_type=MESH,
        ).start()

    def spread(name, count, dev, unit=1):
        for k in far_first(count, unit):
            send(ref[name].at[0], name, k, dev(k))

    def scatter(src, name, count, me, dev, unit=1):
        for k in far_first(count, unit):
            send(ref[src].at[jnp.bitwise_xor(me, k)], name, k - 1, dev(k))

    def arrived(name, lo, hi):
        r = ref[name].at[pl.ds(lo, hi - lo)]
        pltpu.make_async_copy(r, r, rsem.at[index_of[name]]).wait()

    def total(name, count):
        return tree_sum(ref[name][k] for k in range(count))

    fetches = [
        pltpu.make_async_copy(src, dst, lsem.at[i])
        for i, (src, dst) in enumerate(
            ((theta_hbm, theta_v), (disc_hbm, disc_v), (icpt_hbm, icpt_s), (codes_hbm, codes_v))
        )
    ]
    for fetch in fetches[:3]:
        fetch.start()

    barrier = pltpu.get_barrier_semaphore()
    partners = [dev_h(1)] + [dev_yc(k) for k in far_first(NYC, C)]
    partners += [dev_l(k) for k in far_first(ZL)] + [dev_x(k) for k in far_first(X)]
    for partner in partners:
        pl.semaphore_signal(barrier, inc=1, device_id=partner, device_id_type=MESH)
    fetches[3].start()

    low8 = lax.broadcasted_iota(jnp.int32, (8, W), 1) // K
    fetches[0].wait()
    th = theta_v[...]
    ref["t1"][0] = jnp.where(low8 == zh, jnp.concatenate([th, th], 1), 0.0)
    fetches[1].wait()
    dc = disc_v[...]
    ref["d1"][0] = jnp.where(low8 == zq, jnp.concatenate([dc, dc], 1), 0.0)
    fetches[2].wait()
    qlane = lax.broadcasted_iota(jnp.int32, (1, Q), 1)
    brow = jnp.zeros((1, Q), F32)
    for k in range(8):
        brow = jnp.where(qlane == stu * 8 + k, icpt_s[k], brow)
    ref["b1"][0] = brow

    pl.semaphore_wait(barrier, len(partners))

    spread("t1", ZH, dev_h)
    spread("d1", ZL, dev_l)
    spread("b1", ZL, dev_l)

    arrived("d1", 1, ZL)
    slot_l = lambda z: jnp.bitwise_xor(zl, z)
    d_own = jnp.concatenate([ref["d1"][slot_l(r)] + ref["d1"][slot_l(half + r)] for r in range(half)], 0)
    ref["d2"][0] = d_own
    spread("d2", X, dev_x)
    arrived("b1", 1, ZL)
    ref["b2"][0] = total("b1", ZL)
    spread("b2", X, dev_x)
    arrived("t1", 1, ZH)
    t_own = total("t1", ZH)
    ref["t2"][0] = t_own
    spread("t2", NYC, dev_yc, C)

    def rows_of(name):
        return jnp.concatenate([ref[name][jnp.bitwise_xor(yc, k)] for k in range(NYC)], 0)

    def low(v):
        return lax.broadcasted_iota(jnp.int32, v.shape, 1) < K

    def swap(v):
        return pltpu.roll(v, K, 1)

    def cols_of(name):
        packed = jnp.concatenate(
            [ref[name][jnp.bitwise_xor(x, k), pl.ds(r * 8, 8)] for r in range(half) for k in range(X)], 0
        )
        turned = swap(packed)
        lo = low(packed)
        zero = jnp.zeros_like(packed)
        first = jnp.concatenate([jnp.where(lo, packed, zero), jnp.where(lo, turned, zero)], 0)
        second = jnp.concatenate([jnp.where(lo, zero, turned), jnp.where(lo, zero, packed)], 0)
        return first, second

    def pack_cols(v):
        upper, lower = v[: Q // 2], v[Q // 2 :]
        return jnp.where(low(upper), upper, lower)

    arrived("d2", 1, X)
    dd = cols_of("d2")
    arrived("b2", 1, X)
    bias = total("b2", X)
    fetches[3].wait()
    arrived("t2", 1, NYC)
    theta = rows_of("t2")
    turned = swap(theta)
    lo = low(theta)
    tt = (jnp.where(lo, theta, turned), jnp.where(lo, turned, theta))

    theta_s, dd_s, tt_s = split(theta), [split(d) for d in dd], [split(t) for t in tt]

    resid, weight = [], []
    for h in range(ZH):
        prob = jax.nn.sigmoid(dot_nt(theta_s, dd_s[h]) + bias)
        code = codes_v[pl.ds(h * SH, SH)]
        observed = (code > 0).astype(F32)
        correct = (code == 2).astype(F32)
        resid.append(observed * (prob - correct))
        weight.append(observed * prob * (1.0 - prob))

    def row_part(u, d):
        return dot_nn(u[0], d[0]) + dot_nn(u[1], d[1])

    def col_part(u, t):
        return pack_cols(dot_tn(u[0], t[0]) + dot_tn(u[1], t[1]))

    def col_sum(u):
        return jnp.sum(u[0], 0, keepdims=True) + jnp.sum(u[1], 0, keepdims=True)

    def put_rows(name, offset, v):
        for k in range(NYC):
            ref[name][k, pl.ds(offset, 8)] = v[k * 8 : (k + 1) * 8]

    def put_cols(name, offset, v):
        for k in range(X):
            for r in range(half):
                start = (r * X + k) * 8
                ref[name][k, pl.ds(offset + r * 8, 8)] = v[start : start + 8]

    def reduce_all(tag, row_list, col_list, sums, after_first=None, after_second=None):
        for i, pair in enumerate(row_list):
            put_rows("ra" + tag, i * 8, row_part(*pair))
        scatter("ra" + tag, "rb" + tag, NYC, yc, dev_yc, C)
        for i, pair in enumerate(col_list):
            put_cols("ca" + tag, i * XB, col_part(*pair))
        scatter("ca" + tag, "cb" + tag, X, x, dev_x)
        ref["sa" + tag][0] = jnp.concatenate([col_sum(value) for value in sums], 0)
        spread("sa" + tag, X, dev_x)
        if after_first is not None:
            after_first()
        arrived("cb" + tag, 0, X - 1)
        ref["cc" + tag][0] = tree_sum([ref["ca" + tag][x]] + [ref["cb" + tag][k] for k in range(X - 1)])
        spread("cc" + tag, ZL, dev_l)
        arrived("sa" + tag, 1, X)
        ref["sb" + tag][0] = total("sa" + tag, X)
        spread("sb" + tag, ZL, dev_l)
        arrived("rb" + tag, 0, NYC - 1)
        ref["rc" + tag][0] = tree_sum([ref["ra" + tag][yc]] + [ref["rb" + tag][k] for k in range(NYC - 1)])
        spread("rc" + tag, ZH, dev_h)
        if after_second is not None:
            after_second()
        arrived("cc" + tag, 1, ZL)
        cols = total("cc" + tag, ZL)
        arrived("sb" + tag, 1, ZL)
        sums = total("sb" + tag, ZL)
        arrived("rc" + tag, 1, ZH)
        rows = total("rc" + tag, ZH)
        return rows, cols, sums

    def gather_start(tag, rows, cols):
        ref["rg" + tag][0] = rows
        spread("rg" + tag, NYC, dev_yc, C)
        ref["cg" + tag][0] = cols
        spread("cg" + tag, X, dev_x)

    def change_of(tag, vb):
        arrived("cg" + tag, 1, X)
        va = cols_of("cg" + tag)
        base = [dot_nt(theta_s, split(va[h])) + vb for h in range(ZH)]
        arrived("rg" + tag, 1, NYC)
        vt = split(rows_of("rg" + tag))
        return [dot_nt(vt, dd_s[h]) + base[h] for h in range(ZH)]

    def lanes(v):
        s = jnp.sum(v, 0, keepdims=True)
        if s.shape[1] < W:
            s = jnp.concatenate([s, jnp.zeros((1, W - s.shape[1]), F32)], 1)
        return s

    def inner(u, v):
        rows = lanes(u[0] * v[0]) * (1.0 / ZH)
        cols = lanes(u[1] * v[1]) * (1.0 / ZL)
        return rows + cols + lanes(u[2] * v[2]) * (1.0 / (ZL * X))

    def first_round(tag, values):
        for i, v in enumerate(values):
            ref["p" + tag][0, pl.ds(i, 1)] = v
        spread("p" + tag, NXY, dev_xy)

    def second_round(tag):
        arrived("p" + tag, 1, NXY)
        ref["q" + tag][0] = jnp.sum(ref["p" + tag][...], 0)
        spread("q" + tag, NZC, dev_zc)

    def last_round(tag):
        arrived("q" + tag, 1, NZC)
        return jnp.sum(jnp.sum(ref["q" + tag][...], 0), 1, keepdims=True)

    d2 = [split(d * d) for d in dd]
    t2 = [split(t * t) for t in tt]
    resid_s, weight_s = [split(u) for u in resid], [split(u) for u in weight]
    rows, cols, sums = reduce_all(
        "1",
        ((resid_s, dd_s), (weight_s, d2)),
        ((resid_s, tt_s), (weight_s, t2)),
        (resid, weight),
    )
    r = (-(rows[:8] + t_own), -(cols[:XB] + d_own), -(sums[0:1] + bias))
    dg = (rows[8:] + 1.0, cols[XB:] + 1.0, sums[1:2] + 1.0)
    z = [a / b for a, b in zip(r, dg)]
    gather_start("1", z[0], z[1])
    change = change_of("1", z[2])
    scaled = [w * c for w, c in zip(weight, change)]
    scaled_s = [split(u) for u in scaled]

    def first_scalars():
        pq_part = lanes(scaled[0] * change[0]) + lanes(scaled[1] * change[1]) + inner(z, z)
        first_round("1", (inner(r, z), pq_part))

    rows, cols, sums = reduce_all(
        "2",
        ((scaled_s, dd_s),),
        ((scaled_s, tt_s),),
        (scaled,),
        first_scalars,
        lambda: second_round("1"),
    )
    image = (rows + z[0], cols + z[1], sums + z[2])
    scaled_image = [a / b for a, b in zip(image, dg)]
    gather_start("2", scaled_image[0], scaled_image[1])
    scalars = last_round("1")
    rz, pq = scalars[0:1], scalars[1:2]
    alpha = rz / pq
    r = [a - alpha * b for a, b in zip(r, image)]
    z_next = [a / b for a, b in zip(r, dg)]
    new_part = inner(r, z_next)
    own_part, cross_part = inner(z_next, z_next), inner(z_next, z)
    for w, c, s in zip(weight, change, change_of("2", scaled_image[2])):
        n = c - alpha * s
        wn = w * n
        own_part = own_part + lanes(wn * n)
        cross_part = cross_part + lanes(wn * c)
    first_round("2", (new_part, own_part, cross_part))
    second_round("2")
    scalars = last_round("2")
    new, own, cross = scalars[0:1], scalars[1:2], scalars[2:3]
    beta = new / rz
    alpha_two = new / (own + 2.0 * beta * cross + beta * beta * pq)
    step = [
        (alpha * a + alpha_two * (b + beta * a)) * jnp.sqrt(d) for a, b, d in zip(z, z_next, dg)
    ]

    out_t[...] = jnp.where(zh == 0, step[0], swap(step[0]))[:, :K]
    ref["xd"][...] = step[1]
    mine = ref["xd"][pl.ds(pl.multiple_of(zr * 8, 8), 8)]
    out_d[...] = jnp.where(zq == 0, mine, swap(mine))[:, :K]
    out_b[...] = pltpu.roll(step[2], lax.rem(Q - stu * 8, Q), 1)[:, :8]

    assert sum(sent) == math.prod(ref["sent"].shape)
    pltpu.make_async_copy(ref["sent"], ref["sent"], ssem).wait()


def hand_over(*refs):
    ins, outs, sems = refs[:3], refs[3:6], refs[6]
    copies = [pltpu.make_async_copy(a, b, sems.at[i]) for i, (a, b) in enumerate(zip(ins, outs))]
    for copy in copies:
        copy.start()
    for copy in copies:
        copy.wait()


def buffers(dims):
    ZL, X, ZH, Y, C = (dims[n] for n in ("ZL", "X", "ZH", "Y", "C"))
    Q, NYC, XB = ZL * X * 8, Y * C, ZL // 2 * 8
    shapes = {
        "t1": (ZH, 8, W), "d1": (ZL, 8, W), "b1": (ZL, 1, Q),
        "t2": (NYC, 8, W), "d2": (X, XB, W), "b2": (X, 1, Q),
    }
    for tag, n in (("1", 2), ("2", 1)):
        shapes["ra" + tag] = (NYC, n * 8, W)
        shapes["rb" + tag] = (NYC - 1, n * 8, W)
        shapes["rc" + tag] = (ZH, n * 8, W)
        shapes["ca" + tag] = (X, n * XB, W)
        shapes["cb" + tag] = (X - 1, n * XB, W)
        shapes["cc" + tag] = (ZL, n * XB, W)
        shapes["sa" + tag] = (X, n, Q)
        shapes["sb" + tag] = (ZL, n, Q)
        shapes["rg" + tag] = (NYC, 8, W)
        shapes["cg" + tag] = (X, XB, W)
    for tag, n in (("1", 2), ("2", 3)):
        shapes["p" + tag] = (X * Y, n, W)
        shapes["q" + tag] = (ZL * ZH * C, n, W)
    rows, cols = (NYC - 1) * 8 * W, (X - 1) * XB * W
    small = (ZH - 1) * 8 * W + (ZL - 1) * XB * W
    sent = (ZH + ZL - 2) * 8 * W + 6 * (rows + cols) + 3 * small
    sent += 4 * (ZL + X - 2) * Q + 5 * (X * Y + ZL * ZH * C - 2) * W
    shapes["xd"] = (XB, W)
    shapes["sent"] = (sent // Q, 1, Q)
    return shapes


def shards(dims, codes, theta, disc, intercept):
    shapes = buffers(dims)
    names = tuple(shapes)
    made = (
        jax.ShapeDtypeStruct(theta.shape, F32),
        jax.ShapeDtypeStruct(disc.shape, F32),
        jax.ShapeDtypeStruct((1, intercept.shape[0]), F32),
    )
    hbm, vmem = pl.BlockSpec(memory_space=pltpu.HBM), pl.BlockSpec(memory_space=pltpu.VMEM)
    outs = pl.pallas_call(
        functools.partial(kernel, dims, names),
        out_shape=tuple(pltpu.VMEM(s.shape, F32) for s in made),
        in_specs=[hbm, hbm, hbm, hbm],
        out_specs=(vmem, vmem, vmem),
        scratch_shapes=[pltpu.VMEM(shape, F32) for shape in shapes.values()]
        + [
            pltpu.VMEM(codes.shape, jnp.int32),
            pltpu.VMEM(theta.shape, F32),
            pltpu.VMEM(disc.shape, F32),
            pltpu.SMEM(intercept.shape, F32),
            pltpu.SemaphoreType.DMA,
            pltpu.SemaphoreType.DMA((len(names) - len(LOCAL) - len(SHARED),)),
            pltpu.SemaphoreType.DMA((4,)),
        ],
        compiler_params=pltpu.CompilerParams(collective_id=0, has_side_effects=True, vmem_limit_bytes=32 * 2**20),
    )(*(pltpu.with_memory_space_constraint(a, pltpu.HBM) for a in (codes, theta, disc, intercept)))
    outs = pl.pallas_call(
        hand_over,
        out_shape=tuple(pltpu.HBM(s.shape, F32) for s in made),
        in_specs=[vmem, vmem, vmem],
        out_specs=(hbm, hbm, hbm),
        scratch_shapes=[pltpu.SemaphoreType.DMA((3,))],
        compiler_params=pltpu.CompilerParams(vmem_limit_bytes=2**20),
    )(*outs)
    return outs[0], outs[1], outs[2].reshape(intercept.shape)


def solution(mesh):
    return jax.shard_map(
        functools.partial(shards, DIMS),
        mesh=mesh,
        in_specs=(P("stu", "que"), P(("stu", "que"), None), P(("que", "stu"), None), P(("que", "stu"))),
        out_specs=(P(("stu", "que"), None), P(("que", "stu"), None), P(("que", "stu"))),
        check_vma=False,
    )
```

```python
import functools
import math

import jax
import jax.numpy as jnp
from jax import lax
from jax.experimental import pallas as pl
from jax.experimental.pallas import tpu as pltpu
from jax.sharding import PartitionSpec as P

DIMS = dict(ZL=4, X=4, ZH=2, Y=8, C=2)
K = 64
W = 128
LOCAL = ("ra1", "ca1", "ra2", "ca2", "xd", "sent")
SHARED = {"rb2": "rb1", "cb2": "cb1", "sa2": "sa1", "rg1": "t2", "rg2": "t2", "cg1": "d2", "cg2": "d2"}
MESH = pl.DeviceIdType.MESH
F32 = jnp.float32


def split(v):
    head = v.astype(jnp.bfloat16)
    return head, (v - head.astype(F32)).astype(jnp.bfloat16)


def dot(a, b, ca, cb):
    def one(u, v):
        return lax.dot_general(u, v, (((ca,), (cb,)), ((), ())), preferred_element_type=F32)
    return one(a[0], b[0]) + (one(a[0], b[1]) + one(a[1], b[0]))


def dot_nn(a, b):
    return dot(a, b, 1, 0)


def dot_nt(a, b):
    return dot(a, b, 1, 1)


def dot_tn(a, b):
    return dot(a, b, 0, 0)


def tree_sum(parts):
    parts = list(parts)
    while len(parts) > 1:
        parts = [parts[i] + parts[i + 1] if i + 1 < len(parts) else parts[i] for i in range(0, len(parts), 2)]
    return parts[0]


def far_first(count, unit=1):
    order = {4: 0, 5: 1, 3: 2, 7: 3, 6: 4, 2: 5, 1: 6}
    return sorted(range(1, count), key=lambda k: (order.get(k // unit % 8, 7), -k))


Y_HOPS, X_HOPS = (0, 1, 2, 2, 4, 3, 2, 2), (0, 1, 2, 1)
PLANE = sorted(range(1, 32), key=lambda k: -Y_HOPS[k % 8] - X_HOPS[k // 8])
Z_HOPS = (0, 1, 2, 2, 4, 3, 2, 2)
LINE = sorted(range(1, 16), key=lambda k: -Z_HOPS[k // 2 % 2 * 4 + k // 4] - 0.5 * (k % 2))


def kernel(dims, names, codes_hbm, theta_hbm, disc_hbm, icpt_hbm, out_t, out_d, out_b, *rest):
    ZL, X, ZH, Y, C = (dims[n] for n in ("ZL", "X", "ZH", "Y", "C"))
    ref = dict(zip(names, rest))
    codes_v, theta_v, disc_v, icpt_s, ssem, rsem, lsem = rest[len(names):]
    stu, que = lax.axis_index("stu"), lax.axis_index("que")
    zl, x = stu // X, stu % X
    zh, y, core = que // (Y * C), (que // C) % Y, que % C
    half = ZL // 2
    zq, zr = zl // half, zl % half
    Q = ZL * X * 8
    XB = half * 8
    NYC, NXY, NZC = Y * C, X * Y, ZL * ZH * C
    SH = NYC * 8
    yc = y * C + core

    def at(zl_, x_, zh_, y_, core_):
        return (zl_ * X + x_, (zh_ * Y + y_) * C + core_)

    def dev_yc(k):
        return at(zl, x, zh, jnp.bitwise_xor(y, k // C), jnp.bitwise_xor(core, k % C))

    def dev_x(k):
        return at(zl, jnp.bitwise_xor(x, k), zh, y, core)

    def dev_q(k):
        return at(
            zl, x, jnp.bitwise_xor(zh, k // NYC), jnp.bitwise_xor(y, k // C % Y), jnp.bitwise_xor(core, k % C)
        )

    def dev_h(k):
        return at(zl, x, jnp.bitwise_xor(zh, k), y, core)

    def dev_l(k):
        return at(jnp.bitwise_xor(zl, k), x, zh, y, core)

    def dev_xy(k):
        return at(zl, jnp.bitwise_xor(x, k // Y), zh, jnp.bitwise_xor(y, k % Y), core)

    def dev_zc(k):
        return at(
            jnp.bitwise_xor(zl, k // (ZH * C)), x, jnp.bitwise_xor(zh, (k // C) % ZH), y, jnp.bitwise_xor(core, k % C)
        )

    serial = sorted({SHARED.get(n, n) for n in names if n not in LOCAL})
    index_of = {n: serial.index(SHARED.get(n, n)) for n in names if n not in LOCAL}
    sent = []

    def send(src, name, slot, device):
        sent.append(math.prod(src.shape))
        pltpu.make_async_remote_copy(
            src_ref=src,
            dst_ref=ref[name].at[slot],
            send_sem=ssem,
            recv_sem=rsem.at[index_of[name]],
            device_id=device,
            device_id_type=MESH,
        ).start()

    def spread(name, count, dev, unit=1):
        for k in far_first(count, unit):
            send(ref[name].at[0], name, k, dev(k))

    def scatter(src, name, count, me, dev, unit=1):
        for k in far_first(count, unit):
            send(ref[src].at[jnp.bitwise_xor(me, k)], name, k - 1, dev(k))

    def arrived(name, lo, hi):
        r = ref[name].at[pl.ds(lo, hi - lo)]
        pltpu.make_async_copy(r, r, rsem.at[index_of[name]]).wait()

    def total(name, count):
        return tree_sum(ref[name][k] for k in range(count))

    fetches = [
        pltpu.make_async_copy(src, dst, lsem.at[i])
        for i, (src, dst) in enumerate(
            ((theta_hbm, theta_v), (disc_hbm, disc_v), (icpt_hbm, icpt_s), (codes_hbm, codes_v))
        )
    ]
    for fetch in fetches[:3]:
        fetch.start()

    barrier = pltpu.get_barrier_semaphore()
    partners = [dev_h(1)] + [dev_yc(k) for k in far_first(NYC, C)]
    partners += [dev_l(k) for k in far_first(ZL)] + [dev_x(k) for k in far_first(X)]
    for partner in partners:
        pl.semaphore_signal(barrier, inc=1, device_id=partner, device_id_type=MESH)
    fetches[3].start()

    low8 = lax.broadcasted_iota(jnp.int32, (8, W), 1) // K
    fetches[0].wait()
    th = theta_v[...]
    ref["t1"][0] = jnp.where(low8 == zh, jnp.concatenate([th, th], 1), 0.0)
    fetches[1].wait()
    dc = disc_v[...]
    ref["d1"][0] = jnp.where(low8 == zq, jnp.concatenate([dc, dc], 1), 0.0)
    fetches[2].wait()
    qlane = lax.broadcasted_iota(jnp.int32, (1, Q), 1)
    brow = jnp.zeros((1, Q), F32)
    for k in range(8):
        brow = jnp.where(qlane == stu * 8 + k, icpt_s[k], brow)
    ref["b1"][0] = brow

    pl.semaphore_wait(barrier, len(partners))

    spread("t1", ZH, dev_h)
    spread("d1", ZL, dev_l)
    spread("b1", ZL, dev_l)

    arrived("d1", 1, ZL)
    slot_l = lambda z: jnp.bitwise_xor(zl, z)
    d_own = jnp.concatenate([ref["d1"][slot_l(r)] + ref["d1"][slot_l(half + r)] for r in range(half)], 0)
    ref["d2"][0] = d_own
    spread("d2", X, dev_x)
    arrived("b1", 1, ZL)
    ref["b2"][0] = total("b1", ZL)
    spread("b2", X, dev_x)
    arrived("t1", 1, ZH)
    t_own = total("t1", ZH)
    ref["t2"][0] = t_own
    spread("t2", NYC, dev_yc, C)

    def rows_of(name):
        return jnp.concatenate([ref[name][jnp.bitwise_xor(yc, k)] for k in range(NYC)], 0)

    def low(v):
        return lax.broadcasted_iota(jnp.int32, v.shape, 1) < K

    def swap(v):
        return pltpu.roll(v, K, 1)

    def cols_of(name):
        packed = jnp.concatenate(
            [ref[name][jnp.bitwise_xor(x, k), pl.ds(r * 8, 8)] for r in range(half) for k in range(X)], 0
        )
        turned = swap(packed)
        lo = low(packed)
        zero = jnp.zeros_like(packed)
        first = jnp.concatenate([jnp.where(lo, packed, zero), jnp.where(lo, turned, zero)], 0)
        second = jnp.concatenate([jnp.where(lo, zero, turned), jnp.where(lo, zero, packed)], 0)
        return first, second

    def pack_cols(v):
        upper, lower = v[: Q // 2], v[Q // 2 :]
        return jnp.where(low(upper), upper, lower)

    arrived("d2", 1, X)
    dd = cols_of("d2")
    arrived("b2", 1, X)
    bias = total("b2", X)
    fetches[3].wait()
    arrived("t2", 1, NYC)
    theta = rows_of("t2")
    turned = swap(theta)
    lo = low(theta)
    tt = (jnp.where(lo, theta, turned), jnp.where(lo, turned, theta))

    theta_s, dd_s, tt_s = split(theta), [split(d) for d in dd], [split(t) for t in tt]

    resid, weight = [], []
    for h in range(ZH):
        prob = jax.nn.sigmoid(dot_nt(theta_s, dd_s[h]) + bias)
        code = codes_v[pl.ds(h * SH, SH)]
        observed = (code > 0).astype(F32)
        correct = (code == 2).astype(F32)
        resid.append(observed * (prob - correct))
        weight.append(observed * prob * (1.0 - prob))

    def row_part(u, d):
        return dot_nn(u[0], d[0]) + dot_nn(u[1], d[1])

    def col_part(u, t):
        return pack_cols(dot_tn(u[0], t[0]) + dot_tn(u[1], t[1]))

    def col_sum(u):
        return jnp.sum(u[0], 0, keepdims=True) + jnp.sum(u[1], 0, keepdims=True)

    def put_rows(name, offset, v):
        for k in range(NYC):
            ref[name][k, pl.ds(offset, 8)] = v[k * 8 : (k + 1) * 8]

    def put_cols(name, offset, v):
        for k in range(X):
            for r in range(half):
                start = (r * X + k) * 8
                ref[name][k, pl.ds(offset + r * 8, 8)] = v[start : start + 8]

    def reduce_all(tag, row_list, col_list, sums, direct=False, after_first=None, after_second=None):
        for i, pair in enumerate(row_list):
            put_rows("ra" + tag, i * 8, row_part(*pair))
        if direct:
            for k in [NYC + k for k in far_first(NYC, C) + [0]] + far_first(NYC, C):
                send(ref["ra" + tag].at[jnp.bitwise_xor(yc, k % NYC)], "rb" + tag, k - 1, dev_q(k))
        else:
            scatter("ra" + tag, "rb" + tag, NYC, yc, dev_yc, C)
        for i, pair in enumerate(col_list):
            put_cols("ca" + tag, i * XB, col_part(*pair))
        scatter("ca" + tag, "cb" + tag, X, x, dev_x)
        ref["sa" + tag][0] = jnp.concatenate([col_sum(value) for value in sums], 0)
        spread("sa" + tag, X, dev_x)
        if after_first is not None:
            after_first()
        arrived("cb" + tag, 0, X - 1)
        ref["cc" + tag][0] = tree_sum([ref["ca" + tag][x]] + [ref["cb" + tag][k] for k in range(X - 1)])
        spread("cc" + tag, ZL, dev_l)
        arrived("sa" + tag, 1, X)
        ref["sb" + tag][0] = total("sa" + tag, X)
        spread("sb" + tag, ZL, dev_l)
        senders = ZH * NYC - 1 if direct else NYC - 1

        def row_total():
            arrived("rb" + tag, 0, senders)
            return tree_sum([ref["ra" + tag][yc]] + [ref["rb" + tag][k] for k in range(senders)])

        if not direct:
            ref["rc" + tag][0] = row_total()
            spread("rc" + tag, ZH, dev_h)
        if after_second is not None:
            after_second()
        arrived("cc" + tag, 1, ZL)
        cols = total("cc" + tag, ZL)
        arrived("sb" + tag, 1, ZL)
        sums = total("sb" + tag, ZL)
        if direct:
            rows = row_total()
        else:
            arrived("rc" + tag, 1, ZH)
            rows = total("rc" + tag, ZH)
        return rows, cols, sums

    def gather_start(tag, rows, cols):
        ref["rg" + tag][0] = rows
        spread("rg" + tag, NYC, dev_yc, C)
        ref["cg" + tag][0] = cols
        spread("cg" + tag, X, dev_x)

    def change_of(tag, vb):
        arrived("cg" + tag, 1, X)
        va = cols_of("cg" + tag)
        base = [dot_nt(theta_s, split(va[h])) + vb for h in range(ZH)]
        arrived("rg" + tag, 1, NYC)
        vt = split(rows_of("rg" + tag))
        return [dot_nt(vt, dd_s[h]) + base[h] for h in range(ZH)]

    def lanes(v):
        s = jnp.sum(v, 0, keepdims=True)
        if s.shape[1] < W:
            s = jnp.concatenate([s, jnp.zeros((1, W - s.shape[1]), F32)], 1)
        return s

    def inner(u, v):
        rows = lanes(u[0] * v[0]) * (1.0 / ZH)
        cols = lanes(u[1] * v[1]) * (1.0 / ZL)
        return rows + cols + lanes(u[2] * v[2]) * (1.0 / (ZL * X))

    def own_lanes(count):
        group = lax.broadcasted_iota(jnp.int32, (count, W), 1) // 32
        return group == lax.broadcasted_iota(jnp.int32, (count, W), 0)

    def first_round(tag, values):
        stacked = jnp.concatenate(values, 0)
        stacked = stacked + pltpu.roll(stacked, 64, 1)
        stacked = stacked + pltpu.roll(stacked, 32, 1)
        ref["p" + tag][0] = jnp.sum(jnp.where(own_lanes(len(values)), stacked, 0.0), 0, keepdims=True)
        for k in PLANE if NXY == 32 else range(1, NXY):
            send(ref["p" + tag].at[0], "p" + tag, k, dev_xy(k))

    def second_round(tag):
        arrived("p" + tag, 1, NXY)
        ref["q" + tag][0] = jnp.sum(ref["p" + tag][...], 0)
        for k in LINE if NZC == 16 else range(1, NZC):
            send(ref["q" + tag].at[0], "q" + tag, k, dev_zc(k))

    def last_round(tag, count):
        arrived("q" + tag, 1, NZC)
        row = jnp.sum(ref["q" + tag][...], 0)
        return jnp.sum(jnp.where(own_lanes(count), row, 0.0), 1, keepdims=True)

    d2 = [split(d * d) for d in dd]
    t2 = [split(t * t) for t in tt]
    resid_s, weight_s = [split(u) for u in resid], [split(u) for u in weight]
    rows, cols, sums = reduce_all(
        "1",
        ((resid_s, dd_s), (weight_s, d2)),
        ((resid_s, tt_s), (weight_s, t2)),
        (resid, weight),
    )
    r = (-(rows[:8] + t_own), -(cols[:XB] + d_own), -(sums[0:1] + bias))
    dg = (rows[8:] + 1.0, cols[XB:] + 1.0, sums[1:2] + 1.0)
    z = [a / b for a, b in zip(r, dg)]
    gather_start("1", z[0], z[1])
    change = change_of("1", z[2])
    scaled = [w * c for w, c in zip(weight, change)]
    scaled_s = [split(u) for u in scaled]

    def first_scalars():
        pq_part = lanes(scaled[0] * change[0]) + lanes(scaled[1] * change[1]) + inner(z, z)
        first_round("1", (inner(r, z), pq_part))

    rows, cols, sums = reduce_all(
        "2",
        ((scaled_s, dd_s),),
        ((scaled_s, tt_s),),
        (scaled,),
        direct=True,
        after_first=first_scalars,
        after_second=lambda: second_round("1"),
    )
    image = (rows + z[0], cols + z[1], sums + z[2])
    scaled_image = [a / b for a, b in zip(image, dg)]
    gather_start("2", scaled_image[0], scaled_image[1])
    scalars = last_round("1", 2)
    rz, pq = scalars[0:1], scalars[1:2]
    alpha = rz / pq
    r = [a - alpha * b for a, b in zip(r, image)]
    z_next = [a / b for a, b in zip(r, dg)]
    new_part = inner(r, z_next)
    own_part, cross_part = inner(z_next, z_next), inner(z_next, z)
    for w, c, s in zip(weight, change, change_of("2", scaled_image[2])):
        n = c - alpha * s
        wn = w * n
        own_part = own_part + lanes(wn * n)
        cross_part = cross_part + lanes(wn * c)
    first_round("2", (new_part, own_part, cross_part))
    second_round("2")
    scalars = last_round("2", 3)
    new, own, cross = scalars[0:1], scalars[1:2], scalars[2:3]
    beta = new / rz
    alpha_two = new / (own + 2.0 * beta * cross + beta * beta * pq)
    step = [
        (alpha * a + alpha_two * (b + beta * a)) * jnp.sqrt(d) for a, b, d in zip(z, z_next, dg)
    ]

    out_t[...] = jnp.where(zh == 0, step[0], swap(step[0]))[:, :K]
    ref["xd"][...] = step[1]
    mine = ref["xd"][pl.ds(pl.multiple_of(zr * 8, 8), 8)]
    out_d[...] = jnp.where(zq == 0, mine, swap(mine))[:, :K]
    out_b[...] = pltpu.roll(step[2], lax.rem(Q - stu * 8, Q), 1)[:, :8]

    assert sum(sent) == math.prod(ref["sent"].shape)
    pltpu.make_async_copy(ref["sent"], ref["sent"], ssem).wait()


def hand_over(*refs):
    ins, outs, sems = refs[:3], refs[3:6], refs[6]
    copies = [pltpu.make_async_copy(a, b, sems.at[i]) for i, (a, b) in enumerate(zip(ins, outs))]
    for copy in copies:
        copy.start()
    for copy in copies:
        copy.wait()


def buffers(dims):
    ZL, X, ZH, Y, C = (dims[n] for n in ("ZL", "X", "ZH", "Y", "C"))
    Q, NYC, XB = ZL * X * 8, Y * C, ZL // 2 * 8
    shapes = {
        "t1": (ZH, 8, W), "d1": (ZL, 8, W), "b1": (ZL, 1, Q),
        "t2": (NYC, 8, W), "d2": (X, XB, W), "b2": (X, 1, Q),
    }
    for tag, n in (("1", 2), ("2", 1)):
        shapes["ra" + tag] = (NYC, n * 8, W)
        shapes["rb" + tag] = ((NYC if n == 2 else ZH * NYC) - 1, n * 8, W)
        if n == 2:
            shapes["rc" + tag] = (ZH, n * 8, W)
        shapes["ca" + tag] = (X, n * XB, W)
        shapes["cb" + tag] = (X - 1, n * XB, W)
        shapes["cc" + tag] = (ZL, n * XB, W)
        shapes["sa" + tag] = (X, n, Q)
        shapes["sb" + tag] = (ZL, n, Q)
        shapes["rg" + tag] = (NYC, 8, W)
        shapes["cg" + tag] = (X, XB, W)
    for tag in ("1", "2"):
        shapes["p" + tag] = (X * Y, 1, W)
        shapes["q" + tag] = (ZL * ZH * C, 1, W)
    rows, cols = (NYC - 1) * 8 * W, (X - 1) * XB * W
    small = (ZH - 1) * 8 * W + (ZL - 1) * XB * W
    sent = (ZH + ZL - 2) * 8 * W + 7 * rows + 6 * cols + 3 * small
    sent += 4 * (ZL + X - 2) * Q + 2 * (X * Y + ZL * ZH * C - 2) * W
    shapes["xd"] = (XB, W)
    shapes["sent"] = (sent // Q, 1, Q)
    return shapes


def shards(dims, codes, theta, disc, intercept):
    shapes = buffers(dims)
    names = tuple(shapes)
    made = (
        jax.ShapeDtypeStruct(theta.shape, F32),
        jax.ShapeDtypeStruct(disc.shape, F32),
        jax.ShapeDtypeStruct((1, intercept.shape[0]), F32),
    )
    hbm, vmem = pl.BlockSpec(memory_space=pltpu.HBM), pl.BlockSpec(memory_space=pltpu.VMEM)
    outs = pl.pallas_call(
        functools.partial(kernel, dims, names),
        out_shape=tuple(pltpu.VMEM(s.shape, F32) for s in made),
        in_specs=[hbm, hbm, hbm, hbm],
        out_specs=(vmem, vmem, vmem),
        scratch_shapes=[pltpu.VMEM(shape, F32) for shape in shapes.values()]
        + [
            pltpu.VMEM(codes.shape, jnp.int32),
            pltpu.VMEM(theta.shape, F32),
            pltpu.VMEM(disc.shape, F32),
            pltpu.SMEM(intercept.shape, F32),
            pltpu.SemaphoreType.DMA,
            pltpu.SemaphoreType.DMA((len(names) - len(LOCAL) - len(SHARED),)),
            pltpu.SemaphoreType.DMA((4,)),
        ],
        compiler_params=pltpu.CompilerParams(collective_id=0, has_side_effects=True, vmem_limit_bytes=32 * 2**20),
    )(*(pltpu.with_memory_space_constraint(a, pltpu.HBM) for a in (codes, theta, disc, intercept)))
    outs = pl.pallas_call(
        hand_over,
        out_shape=tuple(pltpu.HBM(s.shape, F32) for s in made),
        in_specs=[vmem, vmem, vmem],
        out_specs=(hbm, hbm, hbm),
        scratch_shapes=[pltpu.SemaphoreType.DMA((3,))],
        compiler_params=pltpu.CompilerParams(vmem_limit_bytes=2**20),
    )(*outs)
    return outs[0], outs[1], outs[2].reshape(intercept.shape)


def solution(mesh):
    return jax.shard_map(
        functools.partial(shards, DIMS),
        mesh=mesh,
        in_specs=(P("stu", "que"), P(("stu", "que"), None), P(("que", "stu"), None), P(("que", "stu"))),
        out_specs=(P(("stu", "que"), None), P(("que", "stu"), None), P(("que", "stu"))),
        check_vma=False,
    )
```

```python
import functools
import math

import jax
import jax.numpy as jnp
from jax import lax
from jax.experimental import pallas as pl
from jax.experimental.pallas import tpu as pltpu
from jax.sharding import PartitionSpec as P

DIMS = dict(ZL=4, X=4, ZH=2, Y=8, C=2)
K = 64
W = 128
LOCAL = ("ra1", "ca1", "ra2", "ca2", "xd", "sent")
SHARED = {"rb2": "rb1", "cb2": "cb1", "sa2": "sa1", "rg1": "t2", "rg2": "t2", "cg1": "d2", "cg2": "d2"}
MESH = pl.DeviceIdType.MESH
F32 = jnp.float32


def split(v):
    head = v.astype(jnp.bfloat16)
    return head, (v - head.astype(F32)).astype(jnp.bfloat16)


def dot(a, b, ca, cb):
    def one(u, v):
        return lax.dot_general(u, v, (((ca,), (cb,)), ((), ())), preferred_element_type=F32)
    return one(a[0], b[0]) + (one(a[0], b[1]) + one(a[1], b[0]))


def dot_nn(a, b):
    return dot(a, b, 1, 0)


def dot_nt(a, b):
    return dot(a, b, 1, 1)


def dot_tn(a, b):
    return dot(a, b, 0, 0)


def tree_sum(parts):
    parts = list(parts)
    while len(parts) > 1:
        parts = [parts[i] + parts[i + 1] if i + 1 < len(parts) else parts[i] for i in range(0, len(parts), 2)]
    return parts[0]


def far_first(count, unit=1):
    order = {4: 0, 5: 1, 3: 2, 7: 3, 6: 4, 2: 5, 1: 6}
    return sorted(range(1, count), key=lambda k: (order.get(k // unit % 8, 7), -k))


Y_HOPS, X_HOPS = (0, 1, 2, 2, 4, 3, 2, 2), (0, 1, 2, 1)
PLANE = sorted(range(1, 32), key=lambda k: -Y_HOPS[k % 8] - X_HOPS[k // 8])
Z_HOPS = (0, 1, 2, 2, 4, 3, 2, 2)
LINE = sorted(range(1, 16), key=lambda k: -Z_HOPS[k // 2 % 2 * 4 + k // 4] - 0.5 * (k % 2))


def kernel(dims, names, codes_hbm, theta_hbm, disc_hbm, icpt_hbm, out_t, out_d, out_b, *rest):
    ZL, X, ZH, Y, C = (dims[n] for n in ("ZL", "X", "ZH", "Y", "C"))
    ref = dict(zip(names, rest))
    codes_v, theta_v, disc_v, icpt_s, ssem, rsem, lsem = rest[len(names):]
    stu, que = lax.axis_index("stu"), lax.axis_index("que")
    zl, x = stu // X, stu % X
    zh, y, core = que // (Y * C), (que // C) % Y, que % C
    half = ZL // 2
    zq, zr = zl // half, zl % half
    Q = ZL * X * 8
    XB = half * 8
    NYC, NXY, NZC = Y * C, X * Y, ZL * ZH * C
    SH = NYC * 8
    yc = y * C + core

    def at(zl_, x_, zh_, y_, core_):
        return (zl_ * X + x_, (zh_ * Y + y_) * C + core_)

    def dev_yc(k):
        return at(zl, x, zh, jnp.bitwise_xor(y, k // C), jnp.bitwise_xor(core, k % C))

    def dev_x(k):
        return at(zl, jnp.bitwise_xor(x, k), zh, y, core)

    def dev_q(k):
        return at(
            zl, x, jnp.bitwise_xor(zh, k // NYC), jnp.bitwise_xor(y, k // C % Y), jnp.bitwise_xor(core, k % C)
        )

    def dev_h(k):
        return at(zl, x, jnp.bitwise_xor(zh, k), y, core)

    def dev_l(k):
        return at(jnp.bitwise_xor(zl, k), x, zh, y, core)

    def dev_xy(k):
        return at(zl, jnp.bitwise_xor(x, k // Y), zh, jnp.bitwise_xor(y, k % Y), core)

    def dev_zc(k):
        return at(
            jnp.bitwise_xor(zl, k // (ZH * C)), x, jnp.bitwise_xor(zh, (k // C) % ZH), y, jnp.bitwise_xor(core, k % C)
        )

    serial = sorted({SHARED.get(n, n) for n in names if n not in LOCAL})
    index_of = {n: serial.index(SHARED.get(n, n)) for n in names if n not in LOCAL}
    sent = []

    def send(src, name, slot, device):
        sent.append(math.prod(src.shape))
        pltpu.make_async_remote_copy(
            src_ref=src,
            dst_ref=ref[name].at[slot],
            send_sem=ssem,
            recv_sem=rsem.at[index_of[name]],
            device_id=device,
            device_id_type=MESH,
        ).start()

    def spread(name, count, dev, unit=1):
        for k in far_first(count, unit):
            send(ref[name].at[0], name, k, dev(k))

    def scatter(src, name, count, me, dev, unit=1):
        for k in far_first(count, unit):
            send(ref[src].at[jnp.bitwise_xor(me, k)], name, k - 1, dev(k))

    def arrived(name, lo, hi):
        r = ref[name].at[pl.ds(lo, hi - lo)]
        pltpu.make_async_copy(r, r, rsem.at[index_of[name]]).wait()

    def total(name, count):
        return tree_sum(ref[name][k] for k in range(count))

    fetches = [
        pltpu.make_async_copy(src, dst, lsem.at[i])
        for i, (src, dst) in enumerate(
            ((theta_hbm, theta_v), (disc_hbm, disc_v), (icpt_hbm, icpt_s), (codes_hbm, codes_v))
        )
    ]
    for fetch in fetches[:3]:
        fetch.start()

    barrier = pltpu.get_barrier_semaphore()
    partners = [dev_h(1)] + [dev_yc(k) for k in far_first(NYC, C)]
    partners += [dev_l(k) for k in far_first(ZL)] + [dev_x(k) for k in far_first(X)]
    for partner in partners:
        pl.semaphore_signal(barrier, inc=1, device_id=partner, device_id_type=MESH)
    fetches[3].start()

    low8 = lax.broadcasted_iota(jnp.int32, (8, W), 1) // K
    fetches[0].wait()
    th = theta_v[...]
    ref["t1"][0] = jnp.where(low8 == zh, jnp.concatenate([th, th], 1), 0.0)
    fetches[1].wait()
    dc = disc_v[...]
    ref["d1"][0] = jnp.where(low8 == zq, jnp.concatenate([dc, dc], 1), 0.0)
    fetches[2].wait()
    qlane = lax.broadcasted_iota(jnp.int32, (1, Q), 1)
    brow = jnp.zeros((1, Q), F32)
    for k in range(8):
        brow = jnp.where(qlane == stu * 8 + k, icpt_s[k], brow)
    ref["b1"][0] = brow

    pl.semaphore_wait(barrier, len(partners))

    spread("t1", ZH, dev_h)
    spread("d1", ZL, dev_l)
    spread("b1", ZL, dev_l)

    arrived("t1", 1, ZH)
    t_own = total("t1", ZH)
    ref["t2"][0] = t_own
    spread("t2", NYC, dev_yc, C)
    arrived("d1", 1, ZL)
    slot_l = lambda z: jnp.bitwise_xor(zl, z)
    d_own = jnp.concatenate([ref["d1"][slot_l(r)] + ref["d1"][slot_l(half + r)] for r in range(half)], 0)
    ref["d2"][0] = d_own
    spread("d2", X, dev_x)
    arrived("b1", 1, ZL)
    ref["b2"][0] = total("b1", ZL)
    spread("b2", X, dev_x)

    def rows_of(name):
        return jnp.concatenate([ref[name][jnp.bitwise_xor(yc, k)] for k in range(NYC)], 0)

    def low(v):
        return lax.broadcasted_iota(jnp.int32, v.shape, 1) < K

    def swap(v):
        return pltpu.roll(v, K, 1)

    def cols_of(name):
        packed = jnp.concatenate(
            [ref[name][jnp.bitwise_xor(x, k), pl.ds(r * 8, 8)] for r in range(half) for k in range(X)], 0
        )
        turned = swap(packed)
        lo = low(packed)
        zero = jnp.zeros_like(packed)
        first = jnp.concatenate([jnp.where(lo, packed, zero), jnp.where(lo, turned, zero)], 0)
        second = jnp.concatenate([jnp.where(lo, zero, turned), jnp.where(lo, zero, packed)], 0)
        return first, second

    def pack_cols(v):
        upper, lower = v[: Q // 2], v[Q // 2 :]
        return jnp.where(low(upper), upper, lower)

    arrived("d2", 1, X)
    dd = cols_of("d2")
    arrived("b2", 1, X)
    bias = total("b2", X)
    fetches[3].wait()
    arrived("t2", 1, NYC)
    theta = rows_of("t2")
    turned = swap(theta)
    lo = low(theta)
    tt = (jnp.where(lo, theta, turned), jnp.where(lo, turned, theta))

    theta_s, dd_s, tt_s = split(theta), [split(d) for d in dd], [split(t) for t in tt]

    resid, weight = [], []
    for h in range(ZH):
        prob = jax.nn.sigmoid(dot_nt(theta_s, dd_s[h]) + bias)
        code = codes_v[pl.ds(h * SH, SH)]
        observed = (code > 0).astype(F32)
        correct = (code == 2).astype(F32)
        resid.append(observed * (prob - correct))
        weight.append(observed * prob * (1.0 - prob))

    def row_part(u, d):
        return dot_nn(u[0], d[0]) + dot_nn(u[1], d[1])

    def col_part(u, t):
        return pack_cols(dot_tn(u[0], t[0]) + dot_tn(u[1], t[1]))

    def col_sum(u):
        return jnp.sum(u[0], 0, keepdims=True) + jnp.sum(u[1], 0, keepdims=True)

    def put_rows(name, offset, v):
        for k in range(NYC):
            ref[name][k, pl.ds(offset, 8)] = v[k * 8 : (k + 1) * 8]

    def put_cols(name, offset, v):
        for k in range(X):
            for r in range(half):
                start = (r * X + k) * 8
                ref[name][k, pl.ds(offset + r * 8, 8)] = v[start : start + 8]

    def reduce_all(tag, row_list, col_list, sums, direct=False, after_first=None, after_second=None):
        for i, pair in enumerate(row_list):
            put_rows("ra" + tag, i * 8, row_part(*pair))
        if direct:
            for k in [NYC + k for k in far_first(NYC, C) + [0]] + far_first(NYC, C):
                send(ref["ra" + tag].at[jnp.bitwise_xor(yc, k % NYC)], "rb" + tag, k - 1, dev_q(k))
        else:
            scatter("ra" + tag, "rb" + tag, NYC, yc, dev_yc, C)
        for i, pair in enumerate(col_list):
            put_cols("ca" + tag, i * XB, col_part(*pair))
        scatter("ca" + tag, "cb" + tag, X, x, dev_x)
        ref["sa" + tag][0] = jnp.concatenate([col_sum(value) for value in sums], 0)
        spread("sa" + tag, X, dev_x)
        if after_first is not None:
            after_first()
        arrived("cb" + tag, 0, X - 1)
        ref["cc" + tag][0] = tree_sum([ref["ca" + tag][x]] + [ref["cb" + tag][k] for k in range(X - 1)])
        spread("cc" + tag, ZL, dev_l)
        arrived("sa" + tag, 1, X)
        ref["sb" + tag][0] = total("sa" + tag, X)
        spread("sb" + tag, ZL, dev_l)
        senders = ZH * NYC - 1 if direct else NYC - 1

        def row_total():
            arrived("rb" + tag, 0, senders)
            return tree_sum([ref["ra" + tag][yc]] + [ref["rb" + tag][k] for k in range(senders)])

        if not direct:
            ref["rc" + tag][0] = row_total()
            spread("rc" + tag, ZH, dev_h)
        if after_second is not None:
            after_second()
        arrived("cc" + tag, 1, ZL)
        cols = total("cc" + tag, ZL)
        arrived("sb" + tag, 1, ZL)
        sums = total("sb" + tag, ZL)
        if direct:
            rows = row_total()
        else:
            arrived("rc" + tag, 1, ZH)
            rows = total("rc" + tag, ZH)
        return rows, cols, sums

    def gather_start(tag, rows, cols):
        ref["rg" + tag][0] = rows
        spread("rg" + tag, NYC, dev_yc, C)
        ref["cg" + tag][0] = cols
        spread("cg" + tag, X, dev_x)

    def change_of(tag, vb):
        arrived("cg" + tag, 1, X)
        va = cols_of("cg" + tag)
        base = [dot_nt(theta_s, split(va[h])) + vb for h in range(ZH)]
        arrived("rg" + tag, 1, NYC)
        vt = split(rows_of("rg" + tag))
        return [dot_nt(vt, dd_s[h]) + base[h] for h in range(ZH)]

    def lanes(v):
        s = jnp.sum(v, 0, keepdims=True)
        if s.shape[1] < W:
            s = jnp.concatenate([s, jnp.zeros((1, W - s.shape[1]), F32)], 1)
        return s

    def inner(u, v):
        rows = lanes(u[0] * v[0]) * (1.0 / ZH)
        cols = lanes(u[1] * v[1]) * (1.0 / ZL)
        return rows + cols + lanes(u[2] * v[2]) * (1.0 / (ZL * X))

    def own_lanes(count):
        group = lax.broadcasted_iota(jnp.int32, (count, W), 1) // 32
        return group == lax.broadcasted_iota(jnp.int32, (count, W), 0)

    def first_round(tag, values):
        stacked = jnp.concatenate(values, 0)
        stacked = stacked + pltpu.roll(stacked, 64, 1)
        stacked = stacked + pltpu.roll(stacked, 32, 1)
        ref["p" + tag][0] = jnp.sum(jnp.where(own_lanes(len(values)), stacked, 0.0), 0, keepdims=True)
        for k in PLANE if NXY == 32 else range(1, NXY):
            send(ref["p" + tag].at[0], "p" + tag, k, dev_xy(k))

    def second_round(tag):
        arrived("p" + tag, 1, NXY)
        ref["q" + tag][0] = jnp.sum(ref["p" + tag][...], 0)
        for k in LINE if NZC == 16 else range(1, NZC):
            send(ref["q" + tag].at[0], "q" + tag, k, dev_zc(k))

    def last_round(tag, count):
        arrived("q" + tag, 1, NZC)
        row = jnp.sum(ref["q" + tag][...], 0)
        return jnp.sum(jnp.where(own_lanes(count), row, 0.0), 1, keepdims=True)

    d2 = [split(d * d) for d in dd]
    t2 = [split(t * t) for t in tt]
    resid_s, weight_s = [split(u) for u in resid], [split(u) for u in weight]
    rows, cols, sums = reduce_all(
        "1",
        ((resid_s, dd_s), (weight_s, d2)),
        ((resid_s, tt_s), (weight_s, t2)),
        (resid, weight),
    )
    r = (-(rows[:8] + t_own), -(cols[:XB] + d_own), -(sums[0:1] + bias))
    dg = (rows[8:] + 1.0, cols[XB:] + 1.0, sums[1:2] + 1.0)
    z = [a / b for a, b in zip(r, dg)]
    gather_start("1", z[0], z[1])
    change = change_of("1", z[2])
    scaled = [w * c for w, c in zip(weight, change)]
    scaled_s = [split(u) for u in scaled]

    def first_scalars():
        pq_part = lanes(scaled[0] * change[0]) + lanes(scaled[1] * change[1]) + inner(z, z)
        first_round("1", (inner(r, z), pq_part))

    rows, cols, sums = reduce_all(
        "2",
        ((scaled_s, dd_s),),
        ((scaled_s, tt_s),),
        (scaled,),
        direct=True,
        after_first=first_scalars,
        after_second=lambda: second_round("1"),
    )
    image = (rows + z[0], cols + z[1], sums + z[2])
    scaled_image = [a / b for a, b in zip(image, dg)]
    gather_start("2", scaled_image[0], scaled_image[1])
    scalars = last_round("1", 2)
    rz, pq = scalars[0:1], scalars[1:2]
    alpha = rz / pq
    r = [a - alpha * b for a, b in zip(r, image)]
    z_next = [a / b for a, b in zip(r, dg)]
    new_part = inner(r, z_next)
    own_part, cross_part = inner(z_next, z_next), inner(z_next, z)
    for w, c, s in zip(weight, change, change_of("2", scaled_image[2])):
        n = c - alpha * s
        wn = w * n
        own_part = own_part + lanes(wn * n)
        cross_part = cross_part + lanes(wn * c)
    first_round("2", (new_part, own_part, cross_part))

    root = [jnp.sqrt(d) for d in dg]

    def own_parts(i, p):
        scaled_p = [a * b for a, b in zip(p, root)]
        ref["xd"][i] = scaled_p[1]
        mine = ref["xd"][i, pl.ds(pl.multiple_of(zr * 8, 8), 8)]
        return (
            jnp.where(zh == 0, scaled_p[0], swap(scaled_p[0])),
            jnp.where(zq == 0, mine, swap(mine)),
            pltpu.roll(scaled_p[2], lax.rem(Q - stu * 8, Q), 1),
        )

    parts = list(zip(own_parts(0, z), own_parts(1, z_next)))
    second_round("2")
    scalars = last_round("2", 3)
    new, own, cross = scalars[0:1], scalars[1:2], scalars[2:3]
    beta = new / rz
    alpha_two = new / (own + 2.0 * beta * cross + beta * beta * pq)
    steps = [alpha * a + alpha_two * (b + beta * a) for a, b in parts]
    out_t[...] = steps[0][:, :K]
    out_d[...] = steps[1][:, :K]
    out_b[...] = steps[2][:, :8]

    assert sum(sent) == math.prod(ref["sent"].shape)
    pltpu.make_async_copy(ref["sent"], ref["sent"], ssem).wait()


def hand_over(*refs):
    ins, outs, sems = refs[:3], refs[3:6], refs[6]
    copies = [pltpu.make_async_copy(a, b, sems.at[i]) for i, (a, b) in enumerate(zip(ins, outs))]
    for copy in copies:
        copy.start()
    for copy in copies:
        copy.wait()


def buffers(dims):
    ZL, X, ZH, Y, C = (dims[n] for n in ("ZL", "X", "ZH", "Y", "C"))
    Q, NYC, XB = ZL * X * 8, Y * C, ZL // 2 * 8
    shapes = {
        "t1": (ZH, 8, W), "d1": (ZL, 8, W), "b1": (ZL, 1, Q),
        "t2": (NYC, 8, W), "d2": (X, XB, W), "b2": (X, 1, Q),
    }
    for tag, n in (("1", 2), ("2", 1)):
        shapes["ra" + tag] = (NYC, n * 8, W)
        shapes["rb" + tag] = ((NYC if n == 2 else ZH * NYC) - 1, n * 8, W)
        if n == 2:
            shapes["rc" + tag] = (ZH, n * 8, W)
        shapes["ca" + tag] = (X, n * XB, W)
        shapes["cb" + tag] = (X - 1, n * XB, W)
        shapes["cc" + tag] = (ZL, n * XB, W)
        shapes["sa" + tag] = (X, n, Q)
        shapes["sb" + tag] = (ZL, n, Q)
        shapes["rg" + tag] = (NYC, 8, W)
        shapes["cg" + tag] = (X, XB, W)
    for tag in ("1", "2"):
        shapes["p" + tag] = (X * Y, 1, W)
        shapes["q" + tag] = (ZL * ZH * C, 1, W)
    rows, cols = (NYC - 1) * 8 * W, (X - 1) * XB * W
    small = (ZH - 1) * 8 * W + (ZL - 1) * XB * W
    sent = (ZH + ZL - 2) * 8 * W + 7 * rows + 6 * cols + 3 * small
    sent += 4 * (ZL + X - 2) * Q + 2 * (X * Y + ZL * ZH * C - 2) * W
    shapes["xd"] = (2, XB, W)
    shapes["sent"] = (sent // Q, 1, Q)
    return shapes


def shards(dims, codes, theta, disc, intercept):
    shapes = buffers(dims)
    names = tuple(shapes)
    made = (
        jax.ShapeDtypeStruct(theta.shape, F32),
        jax.ShapeDtypeStruct(disc.shape, F32),
        jax.ShapeDtypeStruct((1, intercept.shape[0]), F32),
    )
    hbm, vmem = pl.BlockSpec(memory_space=pltpu.HBM), pl.BlockSpec(memory_space=pltpu.VMEM)
    outs = pl.pallas_call(
        functools.partial(kernel, dims, names),
        out_shape=tuple(pltpu.VMEM(s.shape, F32) for s in made),
        in_specs=[hbm, hbm, hbm, hbm],
        out_specs=(vmem, vmem, vmem),
        scratch_shapes=[pltpu.VMEM(shape, F32) for shape in shapes.values()]
        + [
            pltpu.VMEM(codes.shape, jnp.int32),
            pltpu.VMEM(theta.shape, F32),
            pltpu.VMEM(disc.shape, F32),
            pltpu.SMEM(intercept.shape, F32),
            pltpu.SemaphoreType.DMA,
            pltpu.SemaphoreType.DMA((len(names) - len(LOCAL) - len(SHARED),)),
            pltpu.SemaphoreType.DMA((4,)),
        ],
        compiler_params=pltpu.CompilerParams(collective_id=0, has_side_effects=True, vmem_limit_bytes=32 * 2**20),
    )(*(pltpu.with_memory_space_constraint(a, pltpu.HBM) for a in (codes, theta, disc, intercept)))
    outs = pl.pallas_call(
        hand_over,
        out_shape=tuple(pltpu.HBM(s.shape, F32) for s in made),
        in_specs=[vmem, vmem, vmem],
        out_specs=(hbm, hbm, hbm),
        scratch_shapes=[pltpu.SemaphoreType.DMA((3,))],
        compiler_params=pltpu.CompilerParams(vmem_limit_bytes=2**20),
    )(*outs)
    return outs[0], outs[1], outs[2].reshape(intercept.shape)


def solution(mesh):
    return jax.shard_map(
        functools.partial(shards, DIMS),
        mesh=mesh,
        in_specs=(P("stu", "que"), P(("stu", "que"), None), P(("que", "stu"), None), P(("que", "stu"))),
        out_specs=(P(("stu", "que"), None), P(("que", "stu"), None), P(("que", "stu"))),
        check_vma=False,
    )
```

```python
import functools
import math

import jax
import jax.numpy as jnp
from jax import lax
from jax.experimental import pallas as pl
from jax.experimental.pallas import tpu as pltpu
from jax.sharding import PartitionSpec as P

DIMS = dict(ZL=4, X=4, ZH=2, Y=8, C=2)
K = 64
W = 128
LOCAL = ("ra1", "ca1", "ra2", "ca2", "xd", "sent")
SHARED = {"rb2": "rb1", "cb2": "cb1", "sa2": "sa1", "rg1": "t2", "rg2": "t2", "cg1": "d2", "cg2": "d2"}
MESH = pl.DeviceIdType.MESH
F32 = jnp.float32


def split(v):
    head = v.astype(jnp.bfloat16)
    return head, (v - head.astype(F32)).astype(jnp.bfloat16)


def dot(a, b, ca, cb):
    def one(u, v):
        return lax.dot_general(u, v, (((ca,), (cb,)), ((), ())), preferred_element_type=F32)
    return one(a[0], b[0]) + (one(a[0], b[1]) + one(a[1], b[0]))


def dot_nn(a, b):
    return dot(a, b, 1, 0)


def dot_nt(a, b):
    return dot(a, b, 1, 1)


def dot_tn(a, b):
    return dot(a, b, 0, 0)


def tree_sum(parts):
    parts = list(parts)
    while len(parts) > 1:
        parts = [parts[i] + parts[i + 1] if i + 1 < len(parts) else parts[i] for i in range(0, len(parts), 2)]
    return parts[0]


def far_first(count, unit=1):
    order = {4: 0, 5: 1, 3: 2, 7: 3, 6: 4, 2: 5, 1: 6}
    return sorted(range(1, count), key=lambda k: (order.get(k // unit % 8, 7), -k))


Y_HOPS, X_HOPS = (0, 1, 2, 2, 4, 3, 2, 2), (0, 1, 2, 1)
PLANE = sorted(range(1, 32), key=lambda k: -Y_HOPS[k % 8] - X_HOPS[k // 8])
Z_HOPS = (0, 1, 2, 2, 4, 3, 2, 2)
LINE = sorted(range(1, 16), key=lambda k: -Z_HOPS[k // 2 % 2 * 4 + k // 4] - 0.5 * (k % 2))


def kernel(dims, names, codes_hbm, theta_hbm, disc_hbm, icpt_hbm, out_t, out_d, out_b, *rest):
    ZL, X, ZH, Y, C = (dims[n] for n in ("ZL", "X", "ZH", "Y", "C"))
    ref = dict(zip(names, rest))
    codes_v, theta_v, disc_v, icpt_s, ssem, rsem, lsem = rest[len(names):]
    stu, que = lax.axis_index("stu"), lax.axis_index("que")
    zl, x = stu // X, stu % X
    zh, y, core = que // (Y * C), (que // C) % Y, que % C
    half = ZL // 2
    zq, zr = zl // half, zl % half
    Q = ZL * X * 8
    XB = half * 8
    NYC, NXY, NZC = Y * C, X * Y, ZL * ZH * C
    SH = NYC * 8
    yc = y * C + core

    def at(zl_, x_, zh_, y_, core_):
        return (zl_ * X + x_, (zh_ * Y + y_) * C + core_)

    def dev_yc(k):
        return at(zl, x, zh, jnp.bitwise_xor(y, k // C), jnp.bitwise_xor(core, k % C))

    def dev_x(k):
        return at(zl, jnp.bitwise_xor(x, k), zh, y, core)

    def dev_q(k):
        return at(
            zl, x, jnp.bitwise_xor(zh, k // NYC), jnp.bitwise_xor(y, k // C % Y), jnp.bitwise_xor(core, k % C)
        )

    def dev_h(k):
        return at(zl, x, jnp.bitwise_xor(zh, k), y, core)

    def dev_l(k):
        return at(jnp.bitwise_xor(zl, k), x, zh, y, core)

    def dev_xy(k):
        return at(zl, jnp.bitwise_xor(x, k // Y), zh, jnp.bitwise_xor(y, k % Y), core)

    def dev_zc(k):
        return at(
            jnp.bitwise_xor(zl, k // (ZH * C)), x, jnp.bitwise_xor(zh, (k // C) % ZH), y, jnp.bitwise_xor(core, k % C)
        )

    serial = sorted({SHARED.get(n, n) for n in names if n not in LOCAL})
    index_of = {n: serial.index(SHARED.get(n, n)) for n in names if n not in LOCAL}
    sent = []

    def send(src, name, slot, device):
        sent.append(math.prod(src.shape))
        pltpu.make_async_remote_copy(
            src_ref=src,
            dst_ref=ref[name].at[slot],
            send_sem=ssem,
            recv_sem=rsem.at[index_of[name]],
            device_id=device,
            device_id_type=MESH,
        ).start()

    def spread(name, count, dev, unit=1):
        for k in far_first(count, unit):
            send(ref[name].at[0], name, k, dev(k))

    def scatter(src, name, count, me, dev, unit=1):
        for k in far_first(count, unit):
            send(ref[src].at[jnp.bitwise_xor(me, k)], name, k - 1, dev(k))

    def arrived(name, lo, hi):
        r = ref[name].at[pl.ds(lo, hi - lo)]
        pltpu.make_async_copy(r, r, rsem.at[index_of[name]]).wait()

    def total(name, count):
        return tree_sum(ref[name][k] for k in range(count))

    fetches = [
        pltpu.make_async_copy(src, dst, lsem.at[i])
        for i, (src, dst) in enumerate(
            ((theta_hbm, theta_v), (disc_hbm, disc_v), (icpt_hbm, icpt_s), (codes_hbm, codes_v))
        )
    ]
    for fetch in fetches[:3]:
        fetch.start()

    barrier = pltpu.get_barrier_semaphore()
    near_y = [dev_yc(k) for k in far_first(NYC, C)]
    near_l = [dev_l(k) for k in far_first(ZL)]
    far = 3 * C
    partners = [dev_h(1)] + near_y[:far] + near_l + near_y[far : 2 * far]
    partners += [dev_x(k) for k in far_first(X)] + near_y[2 * far :]
    for partner in partners:
        pl.semaphore_signal(barrier, inc=1, device_id=partner, device_id_type=MESH)
    fetches[3].start()

    low8 = lax.broadcasted_iota(jnp.int32, (8, W), 1) // K
    fetches[0].wait()
    th = theta_v[...]
    ref["t1"][0] = jnp.where(low8 == zh, jnp.concatenate([th, th], 1), 0.0)
    fetches[1].wait()
    dc = disc_v[...]
    ref["d1"][0] = jnp.where(low8 == zq, jnp.concatenate([dc, dc], 1), 0.0)
    fetches[2].wait()
    qlane = lax.broadcasted_iota(jnp.int32, (1, Q), 1)
    brow = jnp.zeros((1, Q), F32)
    for k in range(8):
        brow = jnp.where(qlane == stu * 8 + k, icpt_s[k], brow)
    ref["b1"][0] = brow

    pl.semaphore_wait(barrier, len(partners))

    spread("t1", ZH, dev_h)
    spread("d1", ZL, dev_l)
    spread("b1", ZL, dev_l)

    arrived("t1", 1, ZH)
    t_own = total("t1", ZH)
    ref["t2"][0] = t_own
    spread("t2", NYC, dev_yc, C)
    arrived("d1", 1, ZL)
    slot_l = lambda z: jnp.bitwise_xor(zl, z)
    d_own = jnp.concatenate([ref["d1"][slot_l(r)] + ref["d1"][slot_l(half + r)] for r in range(half)], 0)
    ref["d2"][0] = d_own
    spread("d2", X, dev_x)
    arrived("b1", 1, ZL)
    ref["b2"][0] = total("b1", ZL)
    spread("b2", X, dev_x)

    def rows_of(name):
        return jnp.concatenate([ref[name][jnp.bitwise_xor(yc, k)] for k in range(NYC)], 0)

    def low(v):
        return lax.broadcasted_iota(jnp.int32, v.shape, 1) < K

    def swap(v):
        return pltpu.roll(v, K, 1)

    def cols_of(name):
        packed = jnp.concatenate(
            [ref[name][jnp.bitwise_xor(x, k), pl.ds(r * 8, 8)] for r in range(half) for k in range(X)], 0
        )
        turned = swap(packed)
        lo = low(packed)
        zero = jnp.zeros_like(packed)
        first = jnp.concatenate([jnp.where(lo, packed, zero), jnp.where(lo, turned, zero)], 0)
        second = jnp.concatenate([jnp.where(lo, zero, turned), jnp.where(lo, zero, packed)], 0)
        return first, second

    def pack_cols(v):
        upper, lower = v[: Q // 2], v[Q // 2 :]
        return jnp.where(low(upper), upper, lower)

    arrived("d2", 1, X)
    dd = cols_of("d2")
    arrived("b2", 1, X)
    bias = total("b2", X)
    fetches[3].wait()
    arrived("t2", 1, NYC)
    theta = rows_of("t2")
    turned = swap(theta)
    lo = low(theta)
    tt = (jnp.where(lo, theta, turned), jnp.where(lo, turned, theta))

    theta_s, dd_s, tt_s = split(theta), [split(d) for d in dd], [split(t) for t in tt]

    resid, weight = [], []
    for h in range(ZH):
        prob = jax.nn.sigmoid(dot_nt(theta_s, dd_s[h]) + bias)
        code = codes_v[pl.ds(h * SH, SH)]
        observed = (code > 0).astype(F32)
        correct = (code == 2).astype(F32)
        resid.append(observed * (prob - correct))
        weight.append(observed * prob * (1.0 - prob))

    def row_part(u, d):
        return dot_nn(u[0], d[0]) + dot_nn(u[1], d[1])

    def col_part(u, t):
        return pack_cols(dot_tn(u[0], t[0]) + dot_tn(u[1], t[1]))

    def col_sum(u):
        return jnp.sum(u[0], 0, keepdims=True) + jnp.sum(u[1], 0, keepdims=True)

    def put_rows(name, offset, v):
        for k in range(NYC):
            ref[name][k, pl.ds(offset, 8)] = v[k * 8 : (k + 1) * 8]

    def put_cols(name, offset, v):
        for k in range(X):
            for r in range(half):
                start = (r * X + k) * 8
                ref[name][k, pl.ds(offset + r * 8, 8)] = v[start : start + 8]

    def reduce_all(tag, row_list, col_list, sums, direct=False, after_first=None, after_second=None):
        for i, pair in enumerate(row_list):
            put_rows("ra" + tag, i * 8, row_part(*pair))
        if direct:
            for k in [NYC + k for k in far_first(NYC, C) + [0]] + far_first(NYC, C):
                send(ref["ra" + tag].at[jnp.bitwise_xor(yc, k % NYC)], "rb" + tag, k - 1, dev_q(k))
        else:
            scatter("ra" + tag, "rb" + tag, NYC, yc, dev_yc, C)
        for i, pair in enumerate(col_list):
            put_cols("ca" + tag, i * XB, col_part(*pair))
        scatter("ca" + tag, "cb" + tag, X, x, dev_x)
        ref["sa" + tag][0] = jnp.concatenate([col_sum(value) for value in sums], 0)
        spread("sa" + tag, X, dev_x)
        if after_first is not None:
            after_first()
        arrived("cb" + tag, 0, X - 1)
        ref["cc" + tag][0] = tree_sum([ref["ca" + tag][x]] + [ref["cb" + tag][k] for k in range(X - 1)])
        spread("cc" + tag, ZL, dev_l)
        arrived("sa" + tag, 1, X)
        ref["sb" + tag][0] = total("sa" + tag, X)
        spread("sb" + tag, ZL, dev_l)
        senders = ZH * NYC - 1 if direct else NYC - 1

        def row_total():
            arrived("rb" + tag, 0, senders)
            return tree_sum([ref["ra" + tag][yc]] + [ref["rb" + tag][k] for k in range(senders)])

        if not direct:
            ref["rc" + tag][0] = row_total()
            spread("rc" + tag, ZH, dev_h)
        if after_second is not None:
            after_second()
        arrived("cc" + tag, 1, ZL)
        cols = total("cc" + tag, ZL)
        arrived("sb" + tag, 1, ZL)
        sums = total("sb" + tag, ZL)
        if direct:
            rows = row_total()
        else:
            arrived("rc" + tag, 1, ZH)
            rows = total("rc" + tag, ZH)
        return rows, cols, sums

    def gather_start(tag, rows, cols):
        ref["rg" + tag][0] = rows
        spread("rg" + tag, NYC, dev_yc, C)
        ref["cg" + tag][0] = cols
        spread("cg" + tag, X, dev_x)

    def change_of(tag, vb):
        arrived("cg" + tag, 1, X)
        va = cols_of("cg" + tag)
        base = [dot_nt(theta_s, split(va[h])) + vb for h in range(ZH)]
        arrived("rg" + tag, 1, NYC)
        vt = split(rows_of("rg" + tag))
        return [dot_nt(vt, dd_s[h]) + base[h] for h in range(ZH)]

    def lanes(v):
        s = jnp.sum(v, 0, keepdims=True)
        if s.shape[1] < W:
            s = jnp.concatenate([s, jnp.zeros((1, W - s.shape[1]), F32)], 1)
        return s

    def inner(u, v):
        rows = lanes(u[0] * v[0]) * (1.0 / ZH)
        cols = lanes(u[1] * v[1]) * (1.0 / ZL)
        return rows + cols + lanes(u[2] * v[2]) * (1.0 / (ZL * X))

    def own_lanes(count):
        group = lax.broadcasted_iota(jnp.int32, (count, W), 1) // 32
        return group == lax.broadcasted_iota(jnp.int32, (count, W), 0)

    def first_round(tag, values):
        stacked = jnp.concatenate(values, 0)
        stacked = stacked + pltpu.roll(stacked, 64, 1)
        stacked = stacked + pltpu.roll(stacked, 32, 1)
        ref["p" + tag][0] = jnp.sum(jnp.where(own_lanes(len(values)), stacked, 0.0), 0, keepdims=True)
        for k in PLANE if NXY == 32 else range(1, NXY):
            send(ref["p" + tag].at[0], "p" + tag, k, dev_xy(k))

    def second_round(tag):
        arrived("p" + tag, 1, NXY)
        ref["q" + tag][0] = jnp.sum(ref["p" + tag][...], 0)
        for k in LINE if NZC == 16 else range(1, NZC):
            send(ref["q" + tag].at[0], "q" + tag, k, dev_zc(k))

    def last_round(tag, count):
        arrived("q" + tag, 1, NZC)
        row = jnp.sum(ref["q" + tag][...], 0)
        return jnp.sum(jnp.where(own_lanes(count), row, 0.0), 1, keepdims=True)

    d2 = [split(d * d) for d in dd]
    t2 = [split(t * t) for t in tt]
    resid_s, weight_s = [split(u) for u in resid], [split(u) for u in weight]
    rows, cols, sums = reduce_all(
        "1",
        ((resid_s, dd_s), (weight_s, d2)),
        ((resid_s, tt_s), (weight_s, t2)),
        (resid, weight),
    )
    r = (-(rows[:8] + t_own), -(cols[:XB] + d_own), -(sums[0:1] + bias))
    dg = (rows[8:] + 1.0, cols[XB:] + 1.0, sums[1:2] + 1.0)
    z = [a / b for a, b in zip(r, dg)]
    gather_start("1", z[0], z[1])
    change = change_of("1", z[2])
    scaled = [w * c for w, c in zip(weight, change)]
    scaled_s = [split(u) for u in scaled]

    def first_scalars():
        pq_part = lanes(scaled[0] * change[0]) + lanes(scaled[1] * change[1]) + inner(z, z)
        first_round("1", (inner(r, z), pq_part))

    rows, cols, sums = reduce_all(
        "2",
        ((scaled_s, dd_s),),
        ((scaled_s, tt_s),),
        (scaled,),
        direct=True,
        after_first=first_scalars,
        after_second=lambda: second_round("1"),
    )
    image = (rows + z[0], cols + z[1], sums + z[2])
    scaled_image = [a / b for a, b in zip(image, dg)]
    gather_start("2", scaled_image[0], scaled_image[1])
    scalars = last_round("1", 2)
    rz, pq = scalars[0:1], scalars[1:2]
    alpha = rz / pq
    r = [a - alpha * b for a, b in zip(r, image)]
    z_next = [a / b for a, b in zip(r, dg)]
    new_part = inner(r, z_next)
    own_part, cross_part = inner(z_next, z_next), inner(z_next, z)
    for w, c, s in zip(weight, change, change_of("2", scaled_image[2])):
        n = c - alpha * s
        wn = w * n
        own_part = own_part + lanes(wn * n)
        cross_part = cross_part + lanes(wn * c)
    first_round("2", (new_part, own_part, cross_part))

    root = [jnp.sqrt(d) for d in dg]

    def own_parts(i, p):
        scaled_p = [a * b for a, b in zip(p, root)]
        ref["xd"][i] = scaled_p[1]
        mine = ref["xd"][i, pl.ds(pl.multiple_of(zr * 8, 8), 8)]
        return (
            jnp.where(zh == 0, scaled_p[0], swap(scaled_p[0])),
            jnp.where(zq == 0, mine, swap(mine)),
            pltpu.roll(scaled_p[2], lax.rem(Q - stu * 8, Q), 1),
        )

    parts = list(zip(own_parts(0, z), own_parts(1, z_next)))
    second_round("2")
    scalars = last_round("2", 3)
    new, own, cross = scalars[0:1], scalars[1:2], scalars[2:3]
    beta = new / rz
    alpha_two = new / (own + 2.0 * beta * cross + beta * beta * pq)
    steps = [alpha * a + alpha_two * (b + beta * a) for a, b in parts]
    out_t[...] = steps[0][:, :K]
    out_d[...] = steps[1][:, :K]
    out_b[...] = steps[2][:, :8]

    assert sum(sent) == math.prod(ref["sent"].shape)
    pltpu.make_async_copy(ref["sent"], ref["sent"], ssem).wait()


def hand_over(*refs):
    ins, outs, sems = refs[:3], refs[3:6], refs[6]
    copies = [pltpu.make_async_copy(a, b, sems.at[i]) for i, (a, b) in enumerate(zip(ins, outs))]
    for copy in copies:
        copy.start()
    for copy in copies:
        copy.wait()


def buffers(dims):
    ZL, X, ZH, Y, C = (dims[n] for n in ("ZL", "X", "ZH", "Y", "C"))
    Q, NYC, XB = ZL * X * 8, Y * C, ZL // 2 * 8
    shapes = {
        "t1": (ZH, 8, W), "d1": (ZL, 8, W), "b1": (ZL, 1, Q),
        "t2": (NYC, 8, W), "d2": (X, XB, W), "b2": (X, 1, Q),
    }
    for tag, n in (("1", 2), ("2", 1)):
        shapes["ra" + tag] = (NYC, n * 8, W)
        shapes["rb" + tag] = ((NYC if n == 2 else ZH * NYC) - 1, n * 8, W)
        if n == 2:
            shapes["rc" + tag] = (ZH, n * 8, W)
        shapes["ca" + tag] = (X, n * XB, W)
        shapes["cb" + tag] = (X - 1, n * XB, W)
        shapes["cc" + tag] = (ZL, n * XB, W)
        shapes["sa" + tag] = (X, n, Q)
        shapes["sb" + tag] = (ZL, n, Q)
        shapes["rg" + tag] = (NYC, 8, W)
        shapes["cg" + tag] = (X, XB, W)
    for tag in ("1", "2"):
        shapes["p" + tag] = (X * Y, 1, W)
        shapes["q" + tag] = (ZL * ZH * C, 1, W)
    rows, cols = (NYC - 1) * 8 * W, (X - 1) * XB * W
    small = (ZH - 1) * 8 * W + (ZL - 1) * XB * W
    sent = (ZH + ZL - 2) * 8 * W + 7 * rows + 6 * cols + 3 * small
    sent += 4 * (ZL + X - 2) * Q + 2 * (X * Y + ZL * ZH * C - 2) * W
    shapes["xd"] = (2, XB, W)
    shapes["sent"] = (sent // Q, 1, Q)
    return shapes


def shards(dims, codes, theta, disc, intercept):
    shapes = buffers(dims)
    names = tuple(shapes)
    made = (
        jax.ShapeDtypeStruct(theta.shape, F32),
        jax.ShapeDtypeStruct(disc.shape, F32),
        jax.ShapeDtypeStruct((1, intercept.shape[0]), F32),
    )
    hbm, vmem = pl.BlockSpec(memory_space=pltpu.HBM), pl.BlockSpec(memory_space=pltpu.VMEM)
    outs = pl.pallas_call(
        functools.partial(kernel, dims, names),
        out_shape=tuple(pltpu.VMEM(s.shape, F32) for s in made),
        in_specs=[hbm, hbm, hbm, hbm],
        out_specs=(vmem, vmem, vmem),
        scratch_shapes=[pltpu.VMEM(shape, F32) for shape in shapes.values()]
        + [
            pltpu.VMEM(codes.shape, jnp.int32),
            pltpu.VMEM(theta.shape, F32),
            pltpu.VMEM(disc.shape, F32),
            pltpu.SMEM(intercept.shape, F32),
            pltpu.SemaphoreType.DMA,
            pltpu.SemaphoreType.DMA((len(names) - len(LOCAL) - len(SHARED),)),
            pltpu.SemaphoreType.DMA((4,)),
        ],
        compiler_params=pltpu.CompilerParams(collective_id=0, has_side_effects=True, vmem_limit_bytes=32 * 2**20),
    )(*(pltpu.with_memory_space_constraint(a, pltpu.HBM) for a in (codes, theta, disc, intercept)))
    outs = pl.pallas_call(
        hand_over,
        out_shape=tuple(pltpu.HBM(s.shape, F32) for s in made),
        in_specs=[vmem, vmem, vmem],
        out_specs=(hbm, hbm, hbm),
        scratch_shapes=[pltpu.SemaphoreType.DMA((3,))],
        compiler_params=pltpu.CompilerParams(vmem_limit_bytes=2**20),
    )(*outs)
    return outs[0], outs[1], outs[2].reshape(intercept.shape)


def solution(mesh):
    return jax.shard_map(
        functools.partial(shards, DIMS),
        mesh=mesh,
        in_specs=(P("stu", "que"), P(("stu", "que"), None), P(("que", "stu"), None), P(("que", "stu"))),
        out_specs=(P(("stu", "que"), None), P(("que", "stu"), None), P(("que", "stu"))),
        check_vma=False,
    )
```
